256 devices in a mesh: scen: 4 (over y), sect: 2 (over core), near: 32 (over z, x).
Axes of the slice: x: 4, y: 4, z: 8, core: 2. Of those that a mesh axis runs over, the one named last changes fastest.
Arguments:
- fields: float32 [20, 1024, 128, 128], P('scen', 'near', 'sect'), parts along dimension 0, may hold values from -6 to 6
- down_state: float32 [12, 4096, 1024], P('scen', 'near', 'sect'), parts along dimension 0, may hold values from -6 to 6
- fire_x: int32 [16], P('scen'), parts along dimension 0, may hold values from 0 to 1023
- hrr_index: int32 [16], P('scen'), parts along dimension 0, may hold values from 0 to 31
- hrr_table: float32 [32], replicated, may hold values from 2 to 20
- profile: float32 [128, 128], P('sect'), may hold values from 0.1 to 1
- courant: float32 [3, 1024], P(None, 'sect'), may hold values from 8 to 262144
- wall_loss: float32 [64, 3, 1024], P(None, None, 'sect'), may hold values from 1e-06 to 0.03
- seg_table: int32 [256], P('near'), may hold values from 0 to 63
Outputs:
- near_next: float32 [20, 1024, 128, 128], P('scen', 'near', 'sect'), parts along dimension 0
- down_next: float32 [12, 4096, 1024], P('scen', 'near', 'sect'), parts along dimension 0
The draws below stay inside these ranges and needn't reach their ends.
There are 4 independent parts, one for each index of `scen`. The reference program is written for one: setup_inputs(seed, part) draws one part's arguments, and reference() takes and returns one part's arrays. A program takes and returns all parts, laid end to end along the dimension named above; an argument that names none is the same for every part. Nothing has to cross between parts.
All inputs are finite; a program needn't handle non-finite values.
Results may differ from the reference program's by a relative error of at most 0.0003.
Values sent between devices are 32-bit elements; how exact they have to be, the bound alone decides.
A program may use at most 128 MiB of HBM per device.

```python
import math
import jax
import jax.numpy as jnp
from jax import lax

NX = 1024
NY = 128
NZ = 128
SEG = 16
WALL_TABLE_ROWS = 64
NFIRE = 4
NSCHED = 32
DX = 4096
DYZ = 1024
NSEG = 256


def draw_courant(key, part):
    lowest = 8.0
    highest = 64.0 * DX
    spread = jax.random.uniform(key, (3, DYZ), jnp.float32)
    return jnp.exp(jnp.log(lowest) + spread * (jnp.log(highest) - jnp.log(lowest)))


def draw_wall_loss(key, part):
    base_key = jax.random.fold_in(key, 11)
    gust_random_key = jax.random.fold_in(key, 12)
    level_key = jax.random.fold_in(key, 13)
    spread = jax.random.uniform(base_key, (WALL_TABLE_ROWS, 3, DYZ), jnp.float32)
    gentle = jnp.exp(jnp.log(1e-06) + spread * (jnp.log(0.0002) - jnp.log(1e-06)))
    gusting_flow = jax.random.uniform(gust_random_key, (WALL_TABLE_ROWS, 1, 1), jnp.float32) < 0.0625
    strong = jax.random.uniform(level_key, (WALL_TABLE_ROWS, 3, DYZ), jnp.float32, minval=0.01, maxval=0.03)
    return jnp.where(gusting_flow, strong, gentle)


def with_ends(entries, key, smallest, top_value):
    extent = entries.shape
    place = [jax.random.randint(jax.random.fold_in(key, axis), (), 0, extent[axis]) for axis in range(len(extent))]
    entries = entries.at[tuple(place)].set(smallest)
    longest = extent.index(max(extent))
    place[longest] = (place[longest] + 1) % extent[longest]
    return entries.at[tuple(place)].set(top_value)


def shard_levels(rng, dims, cuts, low, top_value):
    def one(position, blocks):
        heights = jax.random.uniform(jax.random.fold_in(jax.random.fold_in(rng, 6), position), (blocks,), jnp.float32, low / len(cuts), top_value / len(cuts))
        return jnp.repeat(jnp.exp(heights), dims[position] // blocks).reshape((-1,) + (1,) * (len(dims) - position - 1))

    factor_of = one(*cuts[0])
    for cut in cuts[1:]:
        factor_of = factor_of * one(*cut)
    return factor_of


def centred(key, shape, scale, limit, shards=(), kind=jnp.bfloat16):
    values = scale * jax.random.normal(key, shape, jnp.float32)
    if shards:
        values = values * shard_levels(key, shape, shards, -0.22, 0.18)
    return jnp.clip(values, -limit, limit).astype(kind)


def setup_inputs(seed: int = 0, part: int = 0) -> dict:
    splits = jax.random.split(jax.random.key(seed), 10)
    part_keys = jax.random.split(jax.random.fold_in(splits[9], part), 10)
    fields = centred(part_keys[0], (5, NX, NY, NZ), 1.0, 6.0, ((1, 32), (2, 2)), jnp.float32)
    down_state = centred(part_keys[1], (3, DX, DYZ), 1.0, 6.0, ((1, 32), (2, 2)), jnp.float32)
    fire_x = with_ends(jax.random.randint(part_keys[2], (NFIRE,), 0, NX), jax.random.fold_in(part_keys[2], 1), 0, NX - 1).astype(jnp.int32)
    hrr_index = with_ends(jax.random.randint(part_keys[3], (NFIRE,), 0, NSCHED), jax.random.fold_in(part_keys[3], 1), 0, NSCHED - 1).astype(jnp.int32)
    hrr_table = jnp.clip(jnp.exp(jax.random.uniform(splits[4], (NSCHED,), jnp.float32, math.log(2.0), math.log(20.0))), 2.0, 20.0)
    profile = jnp.clip(jnp.exp(math.log(1.0) - 2.3025851 * jax.random.uniform(splits[5], (NY, NZ), jnp.float32) ** shard_levels(splits[5], (NY, NZ), ((0, 2),), -0.2, 0.2)), 0.1, 1.0)
    courant = draw_courant(jax.random.fold_in(splits[9], 71), part)
    wall_loss = draw_wall_loss(jax.random.fold_in(splits[9], 71), part)
    seg_table = with_ends(jax.random.randint(splits[8], (NSEG,), 0, WALL_TABLE_ROWS), jax.random.fold_in(splits[8], 1), 0, WALL_TABLE_ROWS - 1).astype(jnp.int32)
    return {"fields": fields, "down_state": down_state, "fire_x": fire_x, "hrr_index": hrr_index, "hrr_table": hrr_table, "profile": profile, "courant": courant, "wall_loss": wall_loss, "seg_table": seg_table}


time_step = 0.1
kappa_along = 0.2
diffusivity_depth = 0.2
buoyancy = 0.5
screening = 0.0003
smoke_yield = 0.5
carbon_yield = 0.2
oxygen_yield = 0.3


def sine_rows(length):
    wave_number = jnp.arange(length, dtype=jnp.int32) + 1
    phase_index = (wave_number[:, None] * wave_number[None, :]) % (2 * (length + 1))
    return jnp.sin(jnp.pi * phase_index.astype(jnp.float32) / (length + 1))


def screened_solve(source):
    length = source.shape[0]
    wave_number = (jnp.arange(length, dtype=jnp.int32) + 1).astype(jnp.float32)
    mode_eigenvalue = 2.0 - 2.0 * jnp.cos(jnp.pi * wave_number / (length + 1))
    sine_table = sine_rows(length)
    spectrum = jnp.dot(sine_table, source, precision=lax.Precision.HIGHEST, preferred_element_type=jnp.float32)
    scaled = spectrum / (screening + mode_eigenvalue)[:, None]
    return (2.0 / (length + 1)) * jnp.dot(sine_table, scaled, precision=lax.Precision.HIGHEST, preferred_element_type=jnp.float32)


def advect_species(fields, forward, behind):
    zeros_z = jnp.zeros_like(fields[..., :1])
    upper_z = jnp.concatenate([fields[..., 1:], zeros_z], axis=3)
    lower_z = jnp.concatenate([zeros_z, fields[..., :-1]], axis=3)
    velocity = fields[0:1]
    return (fields - time_step * velocity * (forward - behind) * 0.5
            + kappa_along * (forward - 2.0 * fields + behind)
            + diffusivity_depth * (upper_z - 2.0 * fields + lower_z))


def heat_row(positions, fire_x, hrr_index, hrr_table):
    choose = (hrr_index[:, None] == jnp.arange(hrr_table.shape[0], dtype=jnp.int32)[None, :]).astype(jnp.float32)
    release = jnp.sum(choose * hrr_table[None, :], axis=1)
    at_fire = (positions[:, None] == fire_x[None, :]).astype(jnp.float32)
    return jnp.sum(at_fire * release[None, :], axis=1)


def add_sources(stepped, fields, positions, fire_x, hrr_index, hrr_table, profile):
    heat_rate = heat_row(positions, fire_x, hrr_index, hrr_table)[:, None, None] * profile[None]
    sources = jnp.stack([buoyancy * fields[1], heat_rate, smoke_yield * heat_rate,
                         carbon_yield * heat_rate, -oxygen_yield * heat_rate])
    return stepped + time_step * sources


def coarsen_grid(exit_rows):
    species, height, breadth = exit_rows.shape
    blocks = exit_rows.reshape(species, height // 4, 4, breadth // 4, 4)
    return jnp.mean(blocks, axis=(2, 4)).reshape(species, -1)


def reference(fields, down_state, fire_x, hrr_index, hrr_table, profile, courant, wall_loss, seg_table):
    zeros_x = jnp.zeros_like(fields[:, :1])
    forward = jnp.concatenate([fields[:, 1:], zeros_x], axis=1)
    behind = jnp.concatenate([zeros_x, fields[:, :-1]], axis=1)
    stepped = advect_species(fields, forward, behind)
    positions = jnp.arange(fields.shape[1], dtype=jnp.int32)
    stepped = add_sources(stepped, fields, positions, fire_x, hrr_index, hrr_table, profile)
    ustar = stepped[0]
    behind_u = jnp.concatenate([jnp.zeros_like(ustar[:1]), ustar[:-1]], axis=0)
    source = -(ustar - behind_u)
    pressure = screened_solve(source.reshape(NX, -1)).reshape(ustar.shape)
    forward_p = jnp.concatenate([pressure[1:], jnp.zeros_like(pressure[:1])], axis=0)
    velocity = ustar - (forward_p - pressure)
    near_next = jnp.concatenate([velocity[None], stepped[1:]], axis=0)
    inflow = coarsen_grid(near_next[1:4, -1])
    wall_rows = jnp.moveaxis(wall_loss[jnp.repeat(seg_table, SEG)], 0, 1)
    courant_col = courant[:, None, :]
    factor = 1.0 / ((1.0 + courant_col) * (1.0 + wall_rows))
    decay_rate = courant_col * factor
    forcing = down_state * factor

    def advance(state_now, step_pair):
        state_new = step_pair[0] * state_now + step_pair[1]
        return state_new, state_new

    unused, states = lax.scan(advance, inflow, (jnp.moveaxis(decay_rate, 1, 0), jnp.moveaxis(forcing, 1, 0)))
    down_next = jnp.moveaxis(states, 0, 1)
    return near_next, down_next
```

```python
import math

import jax
import jax.numpy as jnp
from jax import lax
from jax.experimental import pallas as pl
from jax.experimental.pallas import tpu as pltpu
from jax.sharding import PartitionSpec as P

MESH = pl.DeviceIdType.MESH

SEG = 16
time_step = 0.1
kappa_along = 0.2
diffusivity_depth = 0.2
buoyancy = 0.5
screening = 0.0003
source_yields = (0.0, 1.0, 0.5, 0.2, -0.3)

XL = 32
NXD = 4
NZD = 8
LENGTH = XL * NXD * NZD

_t = 2.0 + screening
ROOT = (_t - math.sqrt(_t * _t - 4.0)) / 2.0
GAIN = screening / (1.0 / ROOT - ROOT)


def power(n):
    return ROOT**n


ROUND = 1.0 / (1.0 - power(2 * LENGTH + 2))
GROUP = XL * NXD


def pick(values, index):
    chosen = jnp.float32(values[0])
    for i in range(1, len(values)):
        chosen = jnp.where(index == i, jnp.float32(values[i]), chosen)
    return chosen


def from_below_f(z, s):
    return power(GROUP * (z - 1 - s))


def from_below_b(z, s):
    return power(GROUP * (2 * NZD - 2 - z - s))


def from_above_f(z, s):
    return power(GROUP * (z + s) + 2)


def from_above_b(z, s):
    return power(GROUP * (s - z - 1))


def tunnel_kernel(
    fields, down, fire_x, hrr_index, hrr_table, profile, courant, wall, seg,
    near_out, down_out,
    fbuf, ubuf, halo, dbuf, wallbuf, courbuf, profbuf,
    s1, r1, cross, s2, r2, s3, r3, wseg, fac, rate, pre_a, pre_h,
    fx, hi, ht, sg,
    load_sem, ss1, rs1, ssc, rsc, ssh, rsh, ss2, rs2, ss3, rs3,
):
    me = lax.axis_index("near")
    z = me // NXD
    x = lax.rem(me, NXD)
    rows = fbuf.shape[2]
    quarter = rows // NXD
    spec = dbuf.shape[0]
    chunks = dbuf.shape[1]
    per = spec * chunks // NXD

    def remote(src, dst, send, recv, target):
        return pltpu.make_async_remote_copy(
            src_ref=src, dst_ref=dst, send_sem=send, recv_sem=recv,
            device_id={"near": target}, device_id_type=MESH,
        )

    barrier = pltpu.get_barrier_semaphore()

    def greet(target):
        pl.semaphore_signal(barrier, inc=1, device_id={"near": target}, device_id_type=MESH)

    for k in range(1, NXD):
        greet(z * NXD + lax.rem(x + k, NXD))
    for k in range(1, NZD):
        greet(lax.rem(z + k, NZD) * NXD + x)

    @pl.when(z < NZD - 1)
    def _():
        greet((z + 1) * NXD)

    @pl.when(z > 0)
    def _():
        greet((z - 1) * NXD + NXD - 1)

    loads = [
        pltpu.make_async_copy(src, dst, load_sem.at[i])
        for i, (src, dst) in enumerate((
            (fields.at[pl.ds(0, 1)], fbuf.at[pl.ds(0, 1)]),
            (fields.at[pl.ds(1, 1)], fbuf.at[pl.ds(1, 1)]),
            (seg, sg),
            (fire_x, fx),
            (hrr_index, hi),
            (hrr_table, ht),
            (wall, wallbuf),
            (courant, courbuf),
        ) + tuple((down.at[:, :, pl.ds(128 * c, 128)], dbuf.at[:, c]) for c in range(chunks)) + (
            (fields.at[pl.ds(2, 3)], fbuf.at[pl.ds(2, 3)]),
            (profile, profbuf),
        ))
    ]
    for copy in loads:
        copy.start()

    lane = lax.broadcasted_iota(jnp.int32, (rows, 128), 1)
    not_first = lane > 0
    not_last = lane < 127

    def along_height(f):
        return jnp.where(not_first, pltpu.roll(f, 1, 1), 0.0) + jnp.where(not_last, pltpu.roll(f, 127, 1), 0.0)

    half = 0.5 * time_step
    keep = 1.0 - 2.0 * kappa_along - 2.0 * diffusivity_depth

    loads[0].wait()
    loads[1].wait()

    def velocity(k, ahead, behind):
        u = fbuf[0, k]
        star = keep * u + diffusivity_depth * along_height(u) + (time_step * buoyancy) * fbuf[1, k]
        if ahead is not None:
            star = star + ahead * (kappa_along - half * u)
        if behind is not None:
            star = star + behind * (kappa_along + half * u)
        return star

    star = velocity(0, fbuf[0, 1], None)
    ubuf[0] = star
    near_out[0, 0] = star

    def forward(k, carry):
        f, b, weight = carry
        star = velocity(k, fbuf[0, k + 1], fbuf[0, k - 1])
        f = ROOT * f + star
        ubuf[k] = star
        near_out[0, k] = f
        return f, b + weight * star, weight * ROOT

    f, b, weight = lax.fori_loop(1, XL - 1, forward, (star, star, jnp.float32(ROOT)))
    star = velocity(XL - 1, None, fbuf[0, XL - 2])
    f = ROOT * f + star
    ubuf[XL - 1] = star
    near_out[0, XL - 1] = f
    b = b + power(XL - 1) * star
    for q in range(NXD):
        part = slice(q * quarter, (q + 1) * quarter)
        s1[q, 0:quarter] = f[part]
        s1[q, quarter : 2 * quarter] = b[part]
        s1[q, 2 * quarter : 3 * quarter] = fbuf[0, 0, part]
        s1[q, 3 * quarter : 4 * quarter] = fbuf[0, XL - 1, part]

    for copy in loads[2:-2]:
        copy.wait()
    segments = dbuf.shape[2] // SEG
    for s in range(segments):
        for p in range(spec):
            wseg[p, s : s + 1] = wallbuf[p, pl.ds(sg[s], 1)]
    base_a = 4 * quarter
    base_h = base_a + per
    sub = lax.broadcasted_iota(jnp.int32, (segments, 128), 0)
    for r in range(spec * chunks):
        p, c = divmod(r, chunks)
        cols = slice(c * 128, (c + 1) * 128)
        col = courbuf[p : p + 1, cols]
        factor = 1.0 / ((1.0 + col) * (1.0 + wseg[p, :, cols]))
        a = col * factor
        fac[r] = factor
        rate[r] = a
        h = jnp.zeros((segments, 128), jnp.float32)
        for j in range(SEG):
            h = a * h + factor * dbuf[p, c, pl.ds(j, segments, stride=SEG), :]
        for _ in range(4):
            a = a * a
        for shift in (1, 2, 4):
            ok = sub >= shift
            a_prev = jnp.where(ok, pltpu.roll(a, shift, 0), 1.0)
            h_prev = jnp.where(ok, pltpu.roll(h, shift, 0), 0.0)
            h = a * h_prev + h
            a = a * a_prev
        pre_a[r] = jnp.where(sub >= 1, pltpu.roll(a, 1, 0), 1.0)
        pre_h[r] = jnp.where(sub >= 1, pltpu.roll(h, 1, 0), 0.0)
        q, i = divmod(r, per)
        s1[q, base_a + i : base_a + i + 1] = a[segments - 1 : segments]
        s1[q, base_h + i : base_h + i + 1] = h[segments - 1 : segments]
    for q in range(NXD):
        s1[q, base_h + per :] = jnp.zeros((s1.shape[1] - base_h - per, 128), jnp.float32)

    loads[-2].wait()
    loads[-1].wait()
    first_layer = me * XL

    def heat_at(k):
        total = jnp.float32(0.0)
        for i in range(fx.shape[0]):
            total = total + jnp.where(fx[i] == first_layer + k, ht[hi[i]], 0.0)
        return total * time_step

    def transported(i, k, ahead, behind, heat):
        f = fbuf[i, k]
        return (
            keep * f + diffusivity_depth * along_height(f)
            + kappa_along * (ahead + behind) - half * fbuf[0, k] * (ahead - behind)
            + source_yields[i] * heat
        )

    @pl.when(me == NXD * NZD - 1)
    def _():
        heat = heat_at(XL - 1) * profbuf[...]
        from_lane = lax.broadcasted_iota(jnp.int32, (128, 128), 0)
        to_lane = lax.broadcasted_iota(jnp.int32, (128, 128), 1)
        pool = jnp.where(from_lane // 4 == lax.rem(to_lane, 32), 1.0 / 16.0, 0.0)
        row = lax.broadcasted_iota(jnp.int32, (rows, 128), 0)
        kept = lax.rem(row, 16) // 4 == lane // 32
        for p in range(spec):
            layer = transported(p + 1, XL - 1, jnp.zeros((rows, 128), jnp.float32), fbuf[p + 1, XL - 2], heat)
            pooled = jnp.dot(layer, pool, precision=lax.Precision.HIGHEST, preferred_element_type=jnp.float32)
            pooled = jnp.where(kept, pooled, 0.0)
            for c in range(chunks):
                q, i = divmod(p * chunks + c, per)
                s1[q, base_h + i : base_h + i + 1] = jnp.sum(pooled[16 * c : 16 * c + 16], axis=0, keepdims=True)

    r1[x] = s1[x]

    last_z, last_x = NZD - 1, NXD - 1
    extra = 4 * jnp.where((x == 0) & (z > 0), 1, 0) + 4 * jnp.where((x == last_x) & (z < last_z), 1, 0)
    pl.semaphore_wait(barrier, NXD - 1 + NZD - 1 + extra)

    sends = []
    for k in range(1, NXD):
        to = lax.rem(x + k, NXD)
        copy = remote(s1.at[to], r1.at[x], ss1.at[k - 1], rs1.at[x], z * NXD + to)
        copy.start()
        sends.append(copy)

    def crossing(low):
        side = 2 if low else 3
        target = (z - 1 if low else z + 1) * NXD
        return [
            remote(s1.at[q, pl.ds(side * quarter, quarter)], cross.at[1 if low else 0],
                   ssc.at[0 if low else 1, q], rsc.at[1 if low else 0], target + q)
            for q in range(NXD)
        ]

    @pl.when((x == 0) & (z > 0))
    def _():
        for copy in crossing(True):
            copy.start()

    @pl.when((x == last_x) & (z < last_z))
    def _():
        for copy in crossing(False):
            copy.start()

    up = remote(fbuf.at[:, pl.ds(XL - 1, 1)], halo.at[0], ssh.at[0], rsh.at[0], me + 1)
    low = remote(fbuf.at[:, pl.ds(0, 1)], halo.at[1], ssh.at[1], rsh.at[1], me - 1)
    last = NXD * NZD - 1

    @pl.when(me < last)
    def _():
        up.start()

    @pl.when(me > 0)
    def _():
        low.start()

    def inner(k, carry):
        heat = heat_at(k) * profbuf[...]
        for i in range(1, 5):
            near_out[i, k] = transported(i, k, fbuf[i, k + 1], fbuf[i, k - 1], heat)
        return carry

    lax.fori_loop(1, XL - 1, inner, 0)

    def backward(n, b):
        k = XL - 1 - n
        near_out[0, k] = GAIN * (near_out[0, k] + ROOT * b)
        return ubuf[k] + ROOT * b

    lax.fori_loop(0, XL, backward, jnp.zeros((rows, 128), jnp.float32))

    for k in range(1, NXD):
        source = lax.rem(x + k, NXD)
        remote(r1.at[source], r1.at[source], ss1.at[0], rs1.at[source], me).wait_recv()

    @pl.when(z > 0)
    def _():
        remote(cross.at[0], cross.at[0], ssc.at[0, 0], rsc.at[0], me).wait_recv()

    @pl.when(z == 0)
    def _():
        cross[0] = jnp.zeros((quarter, 128), jnp.float32)

    @pl.when(z < last_z)
    def _():
        remote(cross.at[1], cross.at[1], ssc.at[0, 0], rsc.at[1], me).wait_recv()

    @pl.when(z == last_z)
    def _():
        cross[1] = jnp.zeros((quarter, 128), jnp.float32)

    lows = [r1[i, 2 * quarter : 3 * quarter] for i in range(NXD)]
    highs = [r1[i, 3 * quarter : 4 * quarter] for i in range(NXD)]
    sum_f, sum_b = [], []
    for i in range(NXD):
        before = cross[0] if i == 0 else highs[i - 1]
        after = cross[1] if i == NXD - 1 else lows[i + 1]
        at_low = before * (kappa_along + half * lows[i])
        at_high = after * (kappa_along - half * highs[i])
        sum_f.append(r1[i, 0:quarter] + power(XL - 1) * at_low + at_high)
        sum_b.append(r1[i, quarter : 2 * quarter] + at_low + power(XL - 1) * at_high)
    group_f = sum_f[0]
    for i in range(1, NXD):
        group_f = power(XL) * group_f + sum_f[i]
    group_b = sum_b[NXD - 1]
    for i in reversed(range(NXD - 1)):
        group_b = power(XL) * group_b + sum_b[i]
    rates = [r1[i, base_a : base_a + per] for i in range(NXD)]
    drives = [r1[i, base_h : base_h + per] for i in range(NXD)]
    group_a, group_h = rates[0], drives[0]
    for i in range(1, NXD):
        group_a, group_h = rates[i] * group_a, rates[i] * group_h + drives[i]
    pad = jnp.zeros((s2.shape[1] - quarter - 2 * per, 128), jnp.float32)
    s2[0, 0:quarter] = ROUND * (group_f + pick([power(GROUP + 2 + 2 * GROUP * i) for i in range(NZD)], z) * group_b)
    s2[1, 0:quarter] = ROUND * (group_b + pick([power(GROUP * (2 * NZD - 1) - 2 * GROUP * i) for i in range(NZD)], z) * group_f)
    for side in range(2):
        s2[side, quarter : quarter + per] = group_a
        s2[side, quarter + per : quarter + 2 * per] = jnp.where(z == last_z, drives[NXD - 1], group_h)
        s2[side, quarter + 2 * per :] = pad
    for k in range(1, NZD):
        to = lax.rem(z + k, NZD)
        side = jnp.where(to > z, 0, 1)
        copy = remote(s2.at[side], r2.at[z], ss2.at[k - 1], rs2.at[z], to * NXD + x)
        copy.start()
        sends.append(copy)
    r2[z] = s2[0]

    @pl.when(me > 0)
    def _():
        remote(halo.at[0], halo.at[0], ssh.at[0], rsh.at[0], me).wait_recv()

    @pl.when(me == 0)
    def _():
        halo[0] = jnp.zeros(halo.shape[1:], jnp.float32)

    @pl.when(me < last)
    def _():
        remote(halo.at[1], halo.at[1], ssh.at[0], rsh.at[1], me).wait_recv()

    @pl.when(me == last)
    def _():
        halo[1] = jnp.zeros(halo.shape[1:], jnp.float32)

    heat_low = heat_at(0) * profbuf[...]
    heat_high = heat_at(XL - 1) * profbuf[...]
    for i in range(1, 5):
        near_out[i, 0] = transported(i, 0, fbuf[i, 1], halo[0, i, 0], heat_low)
        near_out[i, XL - 1] = transported(i, XL - 1, halo[1, i, 0], fbuf[i, XL - 2], heat_high)

    for k in range(1, NZD):
        source = lax.rem(z + k, NZD)
        remote(r2.at[source], r2.at[source], ss2.at[0], rs2.at[source], me).wait_recv()

    in_f = ROUND * (pick([power(2 * GROUP * i + 2) for i in range(NZD)], z) * group_b + power(2 * LENGTH - GROUP + 2) * group_f)
    in_b = ROUND * (pick([power(2 * GROUP * (NZD - 1 - i)) for i in range(NZD)], z) * group_f + power(2 * LENGTH - GROUP + 2) * group_b)
    for s in range(NZD):
        part = r2[s, 0:quarter]
        coef_f = pick([from_below_f(i, s) if s < i else from_above_f(i, s) if s > i else 0.0 for i in range(NZD)], z)
        coef_b = pick([from_below_b(i, s) if s < i else from_above_b(i, s) if s > i else 0.0 for i in range(NZD)], z)
        in_f = in_f + coef_f * part
        in_b = in_b + coef_b * part
    arrive = r2[NZD - 1, quarter + per : quarter + 2 * per]
    for s in range(NZD - 1):
        passed = r2[s, quarter : quarter + per] * arrive + r2[s, quarter + per : quarter + 2 * per]
        arrive = jnp.where(s < z, passed, arrive)
    f_at = in_f
    for i in range(NXD):
        s3[i, 0:quarter] = f_at
        f_at = power(XL) * f_at + sum_f[i]
        s3[i, 2 * quarter : 2 * quarter + per] = arrive
        arrive = rates[i] * arrive + drives[i]
        s3[i, 2 * quarter + per :] = jnp.zeros((s3.shape[1] - 2 * quarter - per, 128), jnp.float32)
    b_at = in_b
    for i in reversed(range(NXD)):
        s3[i, quarter : 2 * quarter] = b_at
        b_at = power(XL) * b_at + sum_b[i]
    for k in range(1, NXD):
        to = lax.rem(x + k, NXD)
        copy = remote(s3.at[to], r3.at[x], ss3.at[k - 1], rs3.at[x], z * NXD + to)
        copy.start()
        sends.append(copy)
    r3[x] = s3[x]

    for k in range(1, NXD):
        source = lax.rem(x + k, NXD)
        remote(r3.at[source], r3.at[source], ss3.at[0], rs3.at[source], me).wait_recv()

    from_low = jnp.concatenate([r3[q, 0:quarter] for q in range(NXD)], axis=0)
    from_high = jnp.concatenate([r3[q, quarter : 2 * quarter] for q in range(NXD)], axis=0)
    from_low = GAIN * (ROOT * from_low + halo[0, 0, 0] * (kappa_along + half * fbuf[0, 0]))
    from_high = GAIN * (ROOT * from_high + halo[1, 0, 0] * (kappa_along - half * fbuf[0, XL - 1]))
    for k in range(XL):
        near_out[0, k] = near_out[0, k] + (power(k) * from_low + power(XL - 1 - k) * from_high)

    for r in range(spec * chunks):
        p, c = divmod(r, chunks)
        q, i = divmod(r, per)
        a, factor = rate[r], fac[r]
        h = pre_a[r] * r3[q, 2 * quarter + i : 2 * quarter + i + 1] + pre_h[r]
        for j in range(SEG):
            at = pl.ds(j, segments, stride=SEG)
            h = a * h + factor * dbuf[p, c, at, :]
            down_out[p, c, at, :] = h

    for copy in sends:
        copy.wait_send()

    @pl.when((x == 0) & (z > 0))
    def _():
        for copy in crossing(True):
            copy.wait_send()

    @pl.when((x == last_x) & (z < last_z))
    def _():
        for copy in crossing(False):
            copy.wait_send()

    @pl.when(me < last)
    def _():
        up.wait_send()

    @pl.when(me > 0)
    def _():
        low.wait_send()


def write_kernel(near_in, down_in, near_out, down_out, sem):
    copies = [
        pltpu.make_async_copy(near_in.at[i, pl.ds(h * 16, 16)], near_out.at[i, pl.ds(h * 16, 16)], sem.at[2 * i + h])
        for i in range(5) for h in range(2)
    ]
    copies += [
        pltpu.make_async_copy(down_in.at[:, c], down_out.at[:, :, pl.ds(128 * c, 128)], sem.at[10 + c])
        for c in range(down_in.shape[1])
    ]
    for copy in copies:
        copy.start()
    for copy in copies:
        copy.wait()


def body(fields, down_state, fire_x, hrr_index, hrr_table, profile, courant, wall_loss, seg_table):
    f32 = jnp.float32
    rows = fields.shape[2]
    quarter = rows // NXD
    spec, cells, columns = down_state.shape
    segments = cells // SEG
    lines = spec * columns // 128
    per = lines // NXD

    def padded(n):
        return -(-n // 8) * 8

    n1, n2, n3 = padded(4 * quarter + 2 * per), padded(quarter + 2 * per), padded(2 * quarter + per)
    vmem, smem, dma = pltpu.VMEM, pltpu.SMEM, pltpu.SemaphoreType.DMA
    hbm = pl.BlockSpec(memory_space=pltpu.HBM)
    in_vmem = pl.BlockSpec(memory_space=pltpu.VMEM)
    chunked = (spec, columns // 128, cells, 128)
    near_v, down_v = pl.pallas_call(
        tunnel_kernel,
        out_shape=(jax.ShapeDtypeStruct(fields.shape, f32), jax.ShapeDtypeStruct(chunked, f32)),
        in_specs=[hbm] * 9,
        out_specs=(in_vmem, in_vmem),
        scratch_shapes=[
            vmem(fields.shape, f32),
            vmem(fields.shape[1:], f32),
            vmem((2, 5, 1, rows, 128), f32),
            vmem(chunked, f32),
            vmem((spec, wall_loss.shape[0], columns), f32),
            vmem(courant.shape, f32),
            vmem(profile.shape, f32),
            vmem((NXD, n1, 128), f32),
            vmem((NXD, n1, 128), f32),
            vmem((2, quarter, 128), f32),
            vmem((2, n2, 128), f32),
            vmem((NZD, n2, 128), f32),
            vmem((NXD, n3, 128), f32),
            vmem((NXD, n3, 128), f32),
            vmem((spec, segments, columns), f32),
            vmem((lines, segments, 128), f32),
            vmem((lines, segments, 128), f32),
            vmem((lines, segments, 128), f32),
            vmem((lines, segments, 128), f32),
            smem(fire_x.shape, jnp.int32),
            smem(hrr_index.shape, jnp.int32),
            smem(hrr_table.shape, f32),
            smem(seg_table.shape, jnp.int32),
            dma((14,)),
            dma((NXD - 1,)),
            dma((NXD,)),
            dma((2, NXD)),
            dma((2,)),
            dma((2,)),
            dma((2,)),
            dma((NZD - 1,)),
            dma((NZD,)),
            dma((NXD - 1,)),
            dma((NXD,)),
        ],
        compiler_params=pltpu.CompilerParams(
            collective_id=0, has_side_effects=True, vmem_limit_bytes=32 * 1024 * 1024
        ),
        name="tunnel_step",
    )(*(pltpu.with_memory_space_constraint(a, pltpu.HBM) for a in (fields, down_state, fire_x, hrr_index, hrr_table, profile, courant, jnp.transpose(wall_loss, (1, 0, 2)), seg_table)))
    return pl.pallas_call(
        write_kernel,
        out_shape=(jax.ShapeDtypeStruct(fields.shape, f32), jax.ShapeDtypeStruct(down_state.shape, f32)),
        in_specs=[in_vmem, in_vmem],
        out_specs=(hbm, hbm),
        scratch_shapes=[dma((14,))],
        compiler_params=pltpu.CompilerParams(vmem_limit_bytes=16 * 1024 * 1024),
        name="write_out",
    )(near_v, down_v)


def solution(mesh):
    placed = (
        P("scen", "near", "sect", None),
        P("scen", "near", "sect"),
        P("scen"),
        P("scen"),
        P(),
        P("sect", None),
        P(None, "sect"),
        P(None, None, "sect"),
        P("near"),
    )
    return jax.shard_map(
        body,
        mesh=mesh,
        in_specs=placed,
        out_specs=(P("scen", "near", "sect", None), P("scen", "near", "sect")),
        check_vma=False,
    )
```

```python
import math

import jax
import jax.numpy as jnp
from jax import lax
from jax.experimental import pallas as pl
from jax.experimental.pallas import tpu as pltpu
from jax.sharding import PartitionSpec as P

MESH = pl.DeviceIdType.MESH

SEG = 16
time_step = 0.1
kappa_along = 0.2
diffusivity_depth = 0.2
buoyancy = 0.5
screening = 0.0003
source_yields = (0.0, 1.0, 0.5, 0.2, -0.3)

XL = 32
NXD = 4
NZD = 8
LENGTH = XL * NXD * NZD

_t = 2.0 + screening
ROOT = (_t - math.sqrt(_t * _t - 4.0)) / 2.0
GAIN = screening / (1.0 / ROOT - ROOT)


def power(n):
    return ROOT**n


ROUND = 1.0 / (1.0 - power(2 * LENGTH + 2))
GROUP = XL * NXD


def pick(values, index):
    chosen = jnp.float32(values[0])
    for i in range(1, len(values)):
        chosen = jnp.where(index == i, jnp.float32(values[i]), chosen)
    return chosen


def from_below_f(z, s):
    return power(GROUP * (z - 1 - s))


def from_below_b(z, s):
    return power(GROUP * (2 * NZD - 2 - z - s))


def from_above_f(z, s):
    return power(GROUP * (z + s) + 2)


def from_above_b(z, s):
    return power(GROUP * (s - z - 1))


def tunnel_kernel(
    fields, down, fire_x, hrr_index, hrr_table, profile, courant, wall, seg,
    near_out, edges, dbuf, fac, rate, start,
    fbuf, ubuf, halo, tail, wallbuf, courbuf, profbuf,
    se, re, s1, r1, cross, s2, r2, s3, r3, d1, e1, d2, e2, d3, e3, wseg, pre_a, pre_h,
    fx, hi, ht, sg,
    load_sem, sse, rse, ss1, rs1, ssc, rsc, ssh, rsh, ss2, rs2, ss3, rs3, sd1, rd1, sd2, rd2, sd3, rd3,
):
    me = lax.axis_index("near")
    z = me // NXD
    x = lax.rem(me, NXD)
    last, last_z, last_x = NXD * NZD - 1, NZD - 1, NXD - 1
    rows = fbuf.shape[2]
    quarter = rows // NXD
    spec = dbuf.shape[0]
    chunks = dbuf.shape[1]
    per = spec * chunks // NXD
    lines = [divmod(r, chunks) for r in range(spec * chunks)]

    def remote(src, dst, send, recv, target):
        return pltpu.make_async_remote_copy(
            src_ref=src, dst_ref=dst, send_sem=send, recv_sem=recv,
            device_id={"near": target}, device_id_type=MESH,
        )

    barrier = pltpu.get_barrier_semaphore()

    def greet(target):
        pl.semaphore_signal(barrier, inc=1, device_id={"near": target}, device_id_type=MESH)

    for k in range(1, NZD):
        greet(lax.rem(z + k, NZD) * NXD + x)
    for k in range(1, NXD):
        greet(z * NXD + lax.rem(x + k, NXD))

    @pl.when(z < last_z)
    def _():
        greet((z + 1) * NXD)

    @pl.when(z > 0)
    def _():
        greet((z - 1) * NXD + last_x)

    half_layers = XL // 2
    loads = [
        pltpu.make_async_copy(src, dst, load_sem.at[i])
        for i, (src, dst) in enumerate(tuple(
            (fields.at[pl.ds(f, 1), pl.ds(h * half_layers, half_layers)], fbuf.at[pl.ds(f, 1), pl.ds(h * half_layers, half_layers)])
            for h in range(2) for f in range(2)
        ) + (
            (seg, sg),
            (courant, courbuf),
            (wall, wallbuf),
        ) + tuple((down.at[:, :, pl.ds(128 * c, 128)], dbuf.at[:, c]) for c in range(chunks)) + (
            (fire_x, fx),
            (hrr_index, hi),
            (hrr_table, ht),
            (profile, profbuf),
            (fields.at[pl.ds(1, spec), pl.ds(XL - 2, 2)], tail),
            (fields.at[pl.ds(2, 3)], fbuf.at[pl.ds(2, 3)]),
        ))
    ]
    for copy in loads:
        copy.start()
    velocity_loads, down_loads, small_loads, load_rest = loads[:4], loads[4:-6], loads[-6:-1], loads[-1]

    lane = lax.broadcasted_iota(jnp.int32, (rows, 128), 1)
    not_first = lane > 0
    not_last = lane < 127

    def along_height(f):
        return jnp.where(not_first, pltpu.roll(f, 1, 1), 0.0) + jnp.where(not_last, pltpu.roll(f, 127, 1), 0.0)

    half = 0.5 * time_step
    keep = 1.0 - 2.0 * kappa_along - 2.0 * diffusivity_depth
    for copy in velocity_loads:
        copy.wait()
    for q in range(NXD):
        part = slice(q * quarter, (q + 1) * quarter)
        se[q, 0:quarter] = fbuf[0, 0, part]
        se[q, quarter : 2 * quarter] = fbuf[0, XL - 1, part]

    def velocity(k, ahead, behind):
        u = fbuf[0, k]
        bend = half * u
        star = (time_step * buoyancy) * fbuf[1, k] + diffusivity_depth * (u + along_height(u))
        if ahead is not None:
            star = star + ahead * (kappa_along - bend)
        if behind is not None:
            star = star + behind * (kappa_along + bend)
        return star

    def two_sided():
        star = velocity(0, fbuf[0, 1], None)
        ubuf[0] = star
        near_out[0, 0] = star

        def forward(n, f):
            for k in (2 * n + 1, 2 * n + 2):
                star = velocity(k, fbuf[0, k + 1], fbuf[0, k - 1])
                f = ROOT * f + star
                ubuf[k] = star
                near_out[0, k] = f
            return f

        f = lax.fori_loop(0, (XL - 2) // 2, forward, star)
        star = velocity(XL - 1, None, fbuf[0, XL - 2])
        ubuf[XL - 1] = star
        near_out[0, XL - 1] = ROOT * f + star

        def backward(n, b):
            for k in (XL - 1 - 2 * n, XL - 2 - 2 * n):
                near_out[0, k] = GAIN * (near_out[0, k] + ROOT * b)
                b = ubuf[k] + ROOT * b
            return b

        lax.fori_loop(0, XL // 2, backward, jnp.zeros((rows, 128), jnp.float32))

    early = z < NZD // 2

    @pl.when(early)
    def _():
        two_sided()

    extra = 4 * jnp.where((x == 0) & (z > 0), 1, 0) + 4 * jnp.where((x == last_x) & (z < last_z), 1, 0)
    pl.semaphore_wait(barrier, NXD - 1 + NZD - 1 + extra)

    sends = []

    def to_row(out, into, send, recv):
        for k in (2, 1, 3):
            to = lax.rem(x + k, NXD)
            copy = remote(out.at[to], into.at[x], send.at[k - 1], recv.at[x], z * NXD + to)
            copy.start()
            sends.append(copy)

    def from_row(into, send, recv):
        for k in range(1, NXD):
            source = lax.rem(x + k, NXD)
            remote(into.at[source], into.at[source], send.at[0], recv.at[source], me).wait_recv()

    def to_column(out, into, send, recv):
        for k in (4, 3, 5, 2, 6, 1, 7):
            to = lax.rem(z + k, NZD)
            copy = remote(out.at[jnp.where(to > z, 0, 1)], into.at[z], send.at[k - 1], recv.at[z], to * NXD + x)
            copy.start()
            sends.append(copy)

    def from_column(into, send, recv):
        for k in range(1, NZD):
            source = lax.rem(z + k, NZD)
            remote(into.at[source], into.at[source], send.at[0], recv.at[source], me).wait_recv()

    def crossing(low):
        target = (z - 1 if low else z + 1) * NXD
        return [
            remote(se.at[q, pl.ds(0 if low else quarter, quarter)], cross.at[1 if low else 0],
                   ssc.at[0 if low else 1, q], rsc.at[1 if low else 0], target + q)
            for q in range(NXD)
        ]

    @pl.when((x == 0) & (z > 0))
    def _():
        for copy in crossing(True):
            copy.start()

    @pl.when((x == last_x) & (z < last_z))
    def _():
        for copy in crossing(False):
            copy.start()

    to_row(se, re, sse, rse)

    block = rows // 2
    for part in range(2):
        at = slice(part * block, (part + 1) * block)
        first = fbuf[0, 0, at]
        behind, here = None, first
        for k in range(XL):
            ahead = fbuf[0, k + 1, at] if k < XL - 1 else None
            if behind is None:
                bent = fbuf[1, k, at] - here * ahead
                up_u, up_b, down_u, down_b = here, bent, here, bent
            else:
                slope = behind if ahead is None else behind - ahead
                bent = fbuf[1, k, at] + here * slope
                up_u, up_b = ROOT * up_u + here, ROOT * up_b + bent
                down_u, down_b = down_u + power(k) * here, down_b + power(k) * bent
            behind, here = here, ahead
        final = behind
        ends = (
            (up_u, up_b, ROOT * (up_u - power(XL - 1) * first) + (1.0 / ROOT) * (up_u - final)),
            (down_u, down_b, (1.0 / ROOT) * (down_u - first) + ROOT * (down_u - power(XL - 1) * final)),
        )
        for side, (plain, bent, shifted) in enumerate(ends):
            inside = lax.broadcasted_iota(jnp.int32, (block, 128), 1)
            high = jnp.where(inside > 0, pltpu.roll(plain, 1, 1), 0.0) + jnp.where(inside < 127, pltpu.roll(plain, 127, 1), 0.0)
            total = half * bent + keep * plain + kappa_along * shifted + diffusivity_depth * high
            for i in range(block // quarter):
                s1[part * (block // quarter) + i, side * quarter : (side + 1) * quarter] = total[i * quarter : (i + 1) * quarter]

    to_row(s1, r1, ss1, rs1)

    for copy in down_loads:
        copy.wait()
    segments = dbuf.shape[2] // SEG
    for s in range(segments):
        for p in range(spec):
            wseg[p, s : s + 1] = wallbuf[p, pl.ds(sg[s], 1)]
    sub = lax.broadcasted_iota(jnp.int32, (segments, 128), 0)
    for r, (p, c) in enumerate(lines):
        cols = slice(c * 128, (c + 1) * 128)
        col = courbuf[p : p + 1, cols]
        factor = 1.0 / ((1.0 + col) * (1.0 + wseg[p, :, cols]))
        fac[r] = factor
        rate[r] = col * factor
    state = [jnp.zeros((segments, 128), jnp.float32) for _ in lines]
    for j in range(SEG):
        for r, (p, c) in enumerate(lines):
            state[r] = rate[r] * state[r] + fac[r] * dbuf[p, c, pl.ds(j, segments, stride=SEG), :]
    passed = [rate[r] for r in range(len(lines))]
    for _ in range(4):
        passed = [a * a for a in passed]
    for shift in (1, 2, 4):
        ok = sub >= shift
        for r in range(len(lines)):
            a_prev = jnp.where(ok, pltpu.roll(passed[r], shift, 0), 1.0)
            h_prev = jnp.where(ok, pltpu.roll(state[r], shift, 0), 0.0)
            state[r] = passed[r] * h_prev + state[r]
            passed[r] = passed[r] * a_prev
    zero_rows = jnp.zeros((d1.shape[1], 128), jnp.float32)
    for q in range(NXD):
        d1[q] = zero_rows
        d3[q] = zero_rows
    for r in range(len(lines)):
        pre_a[r] = jnp.where(sub >= 1, pltpu.roll(passed[r], 1, 0), 1.0)
        pre_h[r] = jnp.where(sub >= 1, pltpu.roll(state[r], 1, 0), 0.0)
        q, i = divmod(r, per)
        d1[q, i : i + 1] = passed[r][segments - 1 : segments]
        d1[q, per + i : per + i + 1] = state[r][segments - 1 : segments]

    for copy in small_loads:
        copy.wait()
    fires = [(fx[i] - me * XL, ht[hi[i]] * time_step) for i in range(fx.shape[0])]

    def heat_at(k):
        total = jnp.float32(0.0)
        for place, release in fires:
            total = total + jnp.where(place == k, release, 0.0)
        return total

    def transported(f, u, ahead, behind, heat):
        bend = half * u
        return ahead * (kappa_along - bend) + behind * (kappa_along + bend) + diffusivity_depth * (f + along_height(f)) + heat

    @pl.when(me == last)
    def _():
        heat = heat_at(XL - 1) * profbuf[...]
        from_lane = lax.broadcasted_iota(jnp.int32, (128, 128), 0)
        to_lane = lax.broadcasted_iota(jnp.int32, (128, 128), 1)
        pool = jnp.where(from_lane // 4 == lax.rem(to_lane, 32), 1.0 / 16.0, 0.0)
        row = lax.broadcasted_iota(jnp.int32, (rows, 128), 0)
        kept = lax.rem(row, 16) // 4 == lane // 32
        for p in range(spec):
            layer = transported(tail[p, 1], fbuf[0, XL - 1], jnp.zeros((rows, 128), jnp.float32), tail[p, 0], source_yields[p + 1] * heat)
            pooled = jnp.dot(layer, pool, precision=lax.Precision.HIGHEST, preferred_element_type=jnp.float32)
            pooled = jnp.where(kept, pooled, 0.0)
            for c in range(chunks):
                q, i = divmod(p * chunks + c, per)
                d1[q, per + i : per + i + 1] = jnp.sum(pooled[16 * c : 16 * c + 16], axis=0, keepdims=True)

    to_row(d1, e1, sd1, rd1)
    re[x] = se[x]
    r1[x] = s1[x]
    e1[x] = d1[x]

    load_rest.wait()

    def inner(members):
        def layer(k):
            heat = heat_at(k)
            u = fbuf[0, k]
            bend = half * u
            before, after = kappa_along + bend, kappa_along - bend
            shape = profbuf[...]
            for i in members:
                f = fbuf[i, k]
                moved = fbuf[i, k + 1] * after + fbuf[i, k - 1] * before + diffusivity_depth * (f + along_height(f))
                near_out[i, k] = moved + (source_yields[i] * heat) * shape

        def pair(n, carry):
            layer(2 * n + 1)
            layer(2 * n + 2)
            return carry

        lax.fori_loop(0, (XL - 2) // 2, pair, 0)

    inner((1, 2))

    from_row(re, sse, rse)

    @pl.when(z > 0)
    def _():
        remote(cross.at[0], cross.at[0], ssc.at[0, 0], rsc.at[0], me).wait_recv()

    @pl.when(z == 0)
    def _():
        cross[0] = jnp.zeros((quarter, 128), jnp.float32)

    @pl.when(z < last_z)
    def _():
        remote(cross.at[1], cross.at[1], ssc.at[0, 0], rsc.at[1], me).wait_recv()

    @pl.when(z == last_z)
    def _():
        cross[1] = jnp.zeros((quarter, 128), jnp.float32)

    from_row(r1, ss1, rs1)
    lows = [re[i, 0:quarter] for i in range(NXD)]
    highs = [re[i, quarter : 2 * quarter] for i in range(NXD)]
    sum_f, sum_b = [], []
    for i in range(NXD):
        before = cross[0] if i == 0 else highs[i - 1]
        after = cross[1] if i == NXD - 1 else lows[i + 1]
        at_low = before * (kappa_along + half * lows[i])
        at_high = after * (kappa_along - half * highs[i])
        sum_f.append(r1[i, 0:quarter] + power(XL - 1) * at_low + at_high)
        sum_b.append(r1[i, quarter : 2 * quarter] + at_low + power(XL - 1) * at_high)
    group_f = sum_f[0]
    for i in range(1, NXD):
        group_f = power(XL) * group_f + sum_f[i]
    group_b = sum_b[NXD - 1]
    for i in reversed(range(NXD - 1)):
        group_b = power(XL) * group_b + sum_b[i]
    s2[0] = ROUND * (group_f + pick([power(GROUP + 2 + 2 * GROUP * i) for i in range(NZD)], z) * group_b)
    s2[1] = ROUND * (group_b + pick([power(GROUP * (2 * NZD - 1) - 2 * GROUP * i) for i in range(NZD)], z) * group_f)
    to_column(s2, r2, ss2, rs2)

    from_row(e1, sd1, rd1)
    rates = [e1[i, 0:per] for i in range(NXD)]
    drives = [e1[i, per : 2 * per] for i in range(NXD)]
    group_a, group_h = rates[0], drives[0]
    for i in range(1, NXD):
        group_a, group_h = rates[i] * group_a, rates[i] * group_h + drives[i]
    for side in range(2):
        d2[side] = zero_rows
        d2[side, 0:per] = group_a
        d2[side, per : 2 * per] = jnp.where(z == last_z, drives[NXD - 1], group_h)
    to_column(d2, e2, sd2, rd2)
    r2[z] = s2[0]
    e2[z] = d2[0]

    up = remote(fbuf.at[:, pl.ds(XL - 1, 1)], halo.at[0], ssh.at[0], rsh.at[0], me + 1)
    low = remote(fbuf.at[:, pl.ds(0, 1)], halo.at[1], ssh.at[1], rsh.at[1], me - 1)

    @pl.when(me < last)
    def _():
        up.start()

    @pl.when(me > 0)
    def _():
        low.start()

    inner((3, 4))

    @pl.when(jnp.logical_not(early))
    def _():
        two_sided()

    from_column(r2, ss2, rs2)
    in_f = ROUND * (pick([power(2 * GROUP * i + 2) for i in range(NZD)], z) * group_b + power(2 * LENGTH - GROUP + 2) * group_f)
    in_b = ROUND * (pick([power(2 * GROUP * (NZD - 1 - i)) for i in range(NZD)], z) * group_f + power(2 * LENGTH - GROUP + 2) * group_b)
    for s in range(NZD):
        part = r2[s]
        coef_f = pick([from_below_f(i, s) if s < i else from_above_f(i, s) if s > i else 0.0 for i in range(NZD)], z)
        coef_b = pick([from_below_b(i, s) if s < i else from_above_b(i, s) if s > i else 0.0 for i in range(NZD)], z)
        in_f = in_f + coef_f * part
        in_b = in_b + coef_b * part
    f_at, b_at = in_f, in_b
    for i in range(NXD):
        s3[i, 0:quarter] = f_at
        f_at = power(XL) * f_at + sum_f[i]
    for i in reversed(range(NXD)):
        s3[i, quarter : 2 * quarter] = b_at
        b_at = power(XL) * b_at + sum_b[i]
    to_row(s3, r3, ss3, rs3)

    from_column(e2, sd2, rd2)
    arrive = e2[last_z, per : 2 * per]
    for s in range(NZD - 1):
        passed_on = e2[s, 0:per] * arrive + e2[s, per : 2 * per]
        arrive = jnp.where(s < z, passed_on, arrive)
    for i in range(NXD):
        d3[i, 0:per] = arrive
        arrive = rates[i] * arrive + drives[i]
    to_row(d3, e3, sd3, rd3)
    r3[x] = s3[x]
    e3[x] = d3[x]

    @pl.when(me > 0)
    def _():
        remote(halo.at[0], halo.at[0], ssh.at[0], rsh.at[0], me).wait_recv()

    @pl.when(me == 0)
    def _():
        halo[0] = jnp.zeros(halo.shape[1:], jnp.float32)

    @pl.when(me < last)
    def _():
        remote(halo.at[1], halo.at[1], ssh.at[0], rsh.at[1], me).wait_recv()

    @pl.when(me == last)
    def _():
        halo[1] = jnp.zeros(halo.shape[1:], jnp.float32)

    heat_low = heat_at(0) * profbuf[...]
    heat_high = heat_at(XL - 1) * profbuf[...]
    for i in range(1, 5):
        near_out[i, 0] = transported(fbuf[i, 0], fbuf[0, 0], fbuf[i, 1], halo[0, i, 0], source_yields[i] * heat_low)
        near_out[i, XL - 1] = transported(fbuf[i, XL - 1], fbuf[0, XL - 1], halo[1, i, 0], fbuf[i, XL - 2], source_yields[i] * heat_high)

    from_row(r3, ss3, rs3)
    from_low = jnp.concatenate([r3[q, 0:quarter] for q in range(NXD)], axis=0)
    from_high = jnp.concatenate([r3[q, quarter : 2 * quarter] for q in range(NXD)], axis=0)
    edges[0] = GAIN * (ROOT * from_low + halo[0, 0, 0] * (kappa_along + half * fbuf[0, 0]))
    edges[1] = GAIN * (ROOT * from_high + halo[1, 0, 0] * (kappa_along - half * fbuf[0, XL - 1]))
    from_row(e3, sd3, rd3)
    for r in range(len(lines)):
        q, i = divmod(r, per)
        start[r] = pre_a[r] * e3[q, i : i + 1] + pre_h[r]

    for copy in sends:
        copy.wait_send()

    @pl.when((x == 0) & (z > 0))
    def _():
        for copy in crossing(True):
            copy.wait_send()

    @pl.when((x == last_x) & (z < last_z))
    def _():
        for copy in crossing(False):
            copy.wait_send()

    @pl.when(me < last)
    def _():
        up.wait_send()

    @pl.when(me > 0)
    def _():
        low.wait_send()


def write_kernel(near_in, edges, dbuf, fac, rate, start, near_out, down_out, velocity, dnext, sem):
    copies = [
        pltpu.make_async_copy(near_in.at[i, pl.ds(h * 16, 16)], near_out.at[i, pl.ds(h * 16, 16)], sem.at[2 * i + h])
        for i in range(1, 5) for h in range(2)
    ]
    for copy in copies:
        copy.start()
    spec, chunks = dbuf.shape[:2]
    segments = dbuf.shape[2] // SEG
    for c in range(chunks):
        state = [start[p * chunks + c] for p in range(spec)]
        for j in range(SEG):
            at = pl.ds(j, segments, stride=SEG)
            for p in range(spec):
                r = p * chunks + c
                state[p] = rate[r] * state[p] + fac[r] * dbuf[p, c, at, :]
                dnext[p, c, at, :] = state[p]
        copy = pltpu.make_async_copy(dnext.at[:, c], down_out.at[:, :, pl.ds(128 * c, 128)], sem.at[10 + c])
        copy.start()
        copies.append(copy)
    for part in range(2):
        for k in range(16 * part, 16 * part + 16):
            velocity[k] = near_in[0, k] + (power(k) * edges[0] + power(XL - 1 - k) * edges[1])
        copy = pltpu.make_async_copy(velocity.at[pl.ds(16 * part, 16)], near_out.at[0, pl.ds(16 * part, 16)], sem.at[part])
        copy.start()
        copies.append(copy)
    for copy in copies:
        copy.wait()


def body(fields, down_state, fire_x, hrr_index, hrr_table, profile, courant, wall_loss, seg_table):
    f32 = jnp.float32
    rows = fields.shape[2]
    quarter = rows // NXD
    spec, cells, columns = down_state.shape
    segments = cells // SEG
    lines = spec * columns // 128
    per = lines // NXD

    small = -(-2 * per // 8) * 8
    vmem, smem, dma = pltpu.VMEM, pltpu.SMEM, pltpu.SemaphoreType.DMA
    hbm = pl.BlockSpec(memory_space=pltpu.HBM)
    in_vmem = pl.BlockSpec(memory_space=pltpu.VMEM)
    chunked = (spec, columns // 128, cells, 128)
    shapes = (fields.shape, (2, rows, 128), chunked) + ((lines, segments, 128),) * 3
    middle = pl.pallas_call(
        tunnel_kernel,
        out_shape=tuple(jax.ShapeDtypeStruct(shape, f32) for shape in shapes),
        in_specs=[hbm] * 9,
        out_specs=(in_vmem,) * len(shapes),
        scratch_shapes=[
            vmem(fields.shape, f32),
            vmem(fields.shape[1:], f32),
            vmem((2, 5, 1, rows, 128), f32),
            vmem((spec, 2, rows, 128), f32),
            vmem((spec, wall_loss.shape[0], columns), f32),
            vmem(courant.shape, f32),
            vmem(profile.shape, f32),
            vmem((NXD, 2 * quarter, 128), f32),
            vmem((NXD, 2 * quarter, 128), f32),
            vmem((NXD, 2 * quarter, 128), f32),
            vmem((NXD, 2 * quarter, 128), f32),
            vmem((2, quarter, 128), f32),
            vmem((2, quarter, 128), f32),
            vmem((NZD, quarter, 128), f32),
            vmem((NXD, 2 * quarter, 128), f32),
            vmem((NXD, 2 * quarter, 128), f32),
            vmem((NXD, small, 128), f32),
            vmem((NXD, small, 128), f32),
            vmem((2, small, 128), f32),
            vmem((NZD, small, 128), f32),
            vmem((NXD, small, 128), f32),
            vmem((NXD, small, 128), f32),
            vmem((spec, segments, columns), f32),
            vmem((lines, segments, 128), f32),
            vmem((lines, segments, 128), f32),
            smem(fire_x.shape, jnp.int32),
            smem(hrr_index.shape, jnp.int32),
            smem(hrr_table.shape, f32),
            smem(seg_table.shape, jnp.int32),
            dma((17,)),
            dma((NXD - 1,)),
            dma((NXD,)),
            dma((NXD - 1,)),
            dma((NXD,)),
            dma((2, NXD)),
            dma((2,)),
            dma((2,)),
            dma((2,)),
            dma((NZD - 1,)),
            dma((NZD,)),
            dma((NXD - 1,)),
            dma((NXD,)),
            dma((NXD - 1,)),
            dma((NXD,)),
            dma((NZD - 1,)),
            dma((NZD,)),
            dma((NXD - 1,)),
            dma((NXD,)),
        ],
        compiler_params=pltpu.CompilerParams(
            collective_id=0, has_side_effects=True, vmem_limit_bytes=32 * 1024 * 1024
        ),
        name="tunnel_step",
    )(*(pltpu.with_memory_space_constraint(a, pltpu.HBM) for a in (fields, down_state, fire_x, hrr_index, hrr_table, profile, courant, jnp.transpose(wall_loss, (1, 0, 2)), seg_table)))
    return pl.pallas_call(
        write_kernel,
        out_shape=(jax.ShapeDtypeStruct(fields.shape, f32), jax.ShapeDtypeStruct(down_state.shape, f32)),
        in_specs=[in_vmem] * len(shapes),
        out_specs=(hbm, hbm),
        scratch_shapes=[vmem(fields.shape[1:], f32), vmem(chunked, f32), dma((14,))],
        compiler_params=pltpu.CompilerParams(vmem_limit_bytes=16 * 1024 * 1024),
        name="write_out",
    )(*middle)


def solution(mesh):
    placed = (
        P("scen", "near", "sect", None),
        P("scen", "near", "sect"),
        P("scen"),
        P("scen"),
        P(),
        P("sect", None),
        P(None, "sect"),
        P(None, None, "sect"),
        P("near"),
    )
    return jax.shard_map(
        body,
        mesh=mesh,
        in_specs=placed,
        out_specs=(P("scen", "near", "sect", None), P("scen", "near", "sect")),
        check_vma=False,
    )
```

```python
import math

import jax
import jax.numpy as jnp
from jax import lax
from jax.experimental import pallas as pl
from jax.experimental.pallas import tpu as pltpu
from jax.sharding import PartitionSpec as P

MESH = pl.DeviceIdType.MESH

SEG = 16
time_step = 0.1
kappa_along = 0.2
diffusivity_depth = 0.2
buoyancy = 0.5
screening = 0.0003
source_yields = (0.0, 1.0, 0.5, 0.2, -0.3)

XL = 32
NXD = 4
NZD = 8
LENGTH = XL * NXD * NZD

_t = 2.0 + screening
ROOT = (_t - math.sqrt(_t * _t - 4.0)) / 2.0
GAIN = screening / (1.0 / ROOT - ROOT)


def power(n):
    return ROOT**n


ROUND = 1.0 / (1.0 - power(2 * LENGTH + 2))
GROUP = XL * NXD

FAR = (3, 4, 5)


def pick(values, index):
    chosen = jnp.float32(values[0])
    for i in range(1, len(values)):
        chosen = jnp.where(index == i, jnp.float32(values[i]), chosen)
    return chosen


def from_below_f(z, s):
    return power(GROUP * (z - 1 - s))


def from_below_b(z, s):
    return power(GROUP * (2 * NZD - 2 - z - s))


def from_above_f(z, s):
    return power(GROUP * (z + s) + 2)


def from_above_b(z, s):
    return power(GROUP * (s - z - 1))


def tunnel_kernel(
    fields, down, fire_x, hrr_index, hrr_table, profile, courant, wall, seg,
    near_out, edges, dbuf, fac, rate, start,
    fbuf, ubuf, halo, tail, wallbuf, courbuf, profbuf,
    s1, r1, cross, s2, r2, s3, r3, r4, total, carry, d1, e1, d2, e2, d3, e3, wseg, pre_a, pre_h,
    fx, hi, ht, sg,
    load_sem, ss1, rs1, ssc, rsc, ssh, rsh, ss2, rs2, ss3, rs3, ss4, rs4, sd1, rd1, sd2, rd2, sd3, rd3,
):
    velocity_loads = [pltpu.make_async_copy(fields.at[f], fbuf.at[f], load_sem.at[f]) for f in range(2)]
    for copy in velocity_loads:
        copy.start()
    me = lax.axis_index("near")
    z = me // NXD
    x = lax.rem(me, NXD)
    last, last_z, last_x = NXD * NZD - 1, NZD - 1, NXD - 1
    rows = fbuf.shape[2]
    quarter = rows // NXD
    spec = dbuf.shape[0]
    chunks = dbuf.shape[1]
    per = spec * chunks // NXD
    lines = [divmod(r, chunks) for r in range(spec * chunks)]

    def remote(src, dst, send, recv, target):
        return pltpu.make_async_remote_copy(
            src_ref=src, dst_ref=dst, send_sem=send, recv_sem=recv,
            device_id={"near": target}, device_id_type=MESH,
        )

    barrier = pltpu.get_barrier_semaphore()

    def greet(target):
        pl.semaphore_signal(barrier, inc=1, device_id={"near": target}, device_id_type=MESH)

    for k in (4, 3, 5, 2, 6, 1, 7):
        greet(lax.rem(z + k, NZD) * NXD + x)
    for k in (2, 1, 3):
        greet(z * NXD + lax.rem(x + k, NXD))

    @pl.when(z == 0)
    def _():
        for k in (1, 2, 3):
            for far in FAR:
                greet(far * NXD + lax.rem(x + k, NXD))

    is_far = (z >= FAR[0]) & (z <= FAR[-1])

    @pl.when(z < last_z)
    def _():
        greet((z + 1) * NXD)

    @pl.when(z > 0)
    def _():
        greet((z - 1) * NXD + last_x)

    loads = [
        pltpu.make_async_copy(src, dst, load_sem.at[2 + i])
        for i, (src, dst) in enumerate((
            (seg, sg),
            (courant, courbuf),
            (wall, wallbuf),
        ) + tuple((down.at[:, :, pl.ds(128 * c, 128)], dbuf.at[:, c]) for c in range(chunks)) + (
            (fire_x, fx),
            (hrr_index, hi),
            (hrr_table, ht),
            (profile, profbuf),
            (fields.at[pl.ds(1, spec), pl.ds(XL - 2, 2)], tail),
            (fields.at[pl.ds(2, 3)], fbuf.at[pl.ds(2, 3)]),
        ))
    ]
    for copy in loads:
        copy.start()
    down_loads, small_loads, load_rest = loads[:-6], loads[-6:-1], loads[-1]

    lane = lax.broadcasted_iota(jnp.int32, (rows, 128), 1)
    not_first = lane > 0
    not_last = lane < 127

    def along_height(f):
        return jnp.where(not_first, pltpu.roll(f, 1, 1), 0.0) + jnp.where(not_last, pltpu.roll(f, 127, 1), 0.0)

    half = 0.5 * time_step
    keep = 1.0 - 2.0 * kappa_along - 2.0 * diffusivity_depth
    def velocity(k, ahead, behind):
        u = fbuf[0, k]
        bend = half * u
        star = (time_step * buoyancy) * fbuf[1, k] + diffusivity_depth * (u + along_height(u))
        if ahead is not None:
            star = star + ahead * (kappa_along - bend)
        if behind is not None:
            star = star + behind * (kappa_along + bend)
        return star

    def two_sided():
        star = velocity(0, fbuf[0, 1], None)
        ubuf[0] = star
        near_out[0, 0] = star

        def forward(n, f):
            for k in (2 * n + 1, 2 * n + 2):
                star = velocity(k, fbuf[0, k + 1], fbuf[0, k - 1])
                f = ROOT * f + star
                ubuf[k] = star
                near_out[0, k] = f
            return f

        f = lax.fori_loop(0, (XL - 2) // 2, forward, star)
        star = velocity(XL - 1, None, fbuf[0, XL - 2])
        ubuf[XL - 1] = star
        near_out[0, XL - 1] = ROOT * f + star

        def backward(n, b):
            for k in (XL - 1 - 2 * n, XL - 2 - 2 * n):
                near_out[0, k] = GAIN * (near_out[0, k] + ROOT * b)
                b = ubuf[k] + ROOT * b
            return b

        lax.fori_loop(0, XL // 2, backward, jnp.zeros((rows, 128), jnp.float32))

    early = z < NZD // 2
    for copy in velocity_loads:
        copy.wait()

    @pl.when(early)
    def _():
        two_sided()

    sends = []

    def to_row(out, into, send, recv):
        for k in (2, 1, 3):
            to = lax.rem(x + k, NXD)
            copy = remote(out.at[to], into.at[x], send.at[k - 1], recv.at[x], z * NXD + to)
            copy.start()
            sends.append(copy)

    def from_row(into, send, recv):
        for k in range(1, NXD):
            source = lax.rem(x + k, NXD)
            remote(into.at[source], into.at[source], send.at[0], recv.at[source], me).wait_recv()

    def to_column(out, into, send, recv):
        for k in (4, 3, 5, 2, 6, 1, 7):
            to = lax.rem(z + k, NZD)
            copy = remote(out.at[jnp.where(to > z, 0, 1)], into.at[z], send.at[k - 1], recv.at[z], to * NXD + x)
            copy.start()
            sends.append(copy)

    def from_column(into, send, recv):
        for k in range(1, NZD):
            source = lax.rem(z + k, NZD)
            remote(into.at[source], into.at[source], send.at[0], recv.at[source], me).wait_recv()

    def crossing(low):
        target = (z - 1 if low else z + 1) * NXD
        return [
            remote(s1.at[k, pl.ds((2 if low else 3) * quarter, quarter)], cross.at[1 if low else 0],
                   ssc.at[0 if low else 1, k], rsc.at[1 if low else 0], target + lax.rem(x + k, NXD))
            for k in range(NXD)
        ]

    def columns(turn):
        return pl.ds(pl.multiple_of(lax.rem(x + turn, NXD) * quarter, quarter), quarter)

    for turn in range(NXD):
        s1[turn, 2 * quarter : 3 * quarter] = fbuf[0, 0, columns(turn)]
        s1[turn, 3 * quarter : 4 * quarter] = fbuf[0, XL - 1, columns(turn)]

    inside = lax.broadcasted_iota(jnp.int32, (quarter, 128), 1)

    def local_sums(turns):
        here = {t: fbuf[0, 0, columns(t)] for t in turns}
        behind, total = {}, {}
        for k in range(XL):
            for t in turns:
                ahead = fbuf[0, k + 1, columns(t)] if k < XL - 1 else None
                bent = fbuf[1, k, columns(t)]
                if k == 0:
                    bent = bent - here[t] * ahead
                    total[t] = (here[t], bent, here[t], bent)
                else:
                    bent = bent + here[t] * (behind[t] if ahead is None else behind[t] - ahead)
                    up_u, up_b, down_u, down_b = total[t]
                    total[t] = (ROOT * up_u + here[t], ROOT * up_b + bent, down_u + power(k) * here[t], down_b + power(k) * bent)
                behind[t], here[t] = here[t], ahead
        for t in turns:
            up_u, up_b, down_u, down_b = total[t]
            first, final = fbuf[0, 0, columns(t)], behind[t]
            ends = (
                (up_u, up_b, ROOT * (up_u - power(XL - 1) * first) + (1.0 / ROOT) * (up_u - final)),
                (down_u, down_b, (1.0 / ROOT) * (down_u - first) + ROOT * (down_u - power(XL - 1) * final)),
            )
            for side, (plain, bent, shifted) in enumerate(ends):
                high = jnp.where(inside > 0, pltpu.roll(plain, 1, 1), 0.0) + jnp.where(inside < 127, pltpu.roll(plain, 127, 1), 0.0)
                s1[t, side * quarter : (side + 1) * quarter] = half * bent + keep * plain + kappa_along * shifted + diffusivity_depth * high

    local_sums((2, 1, 3))
    extra = 4 * jnp.where((x == 0) & (z > 0), 1, 0) + 4 * jnp.where((x == last_x) & (z < last_z), 1, 0)
    extra = extra + (NXD - 1) * jnp.where(is_far, 1, 0)
    pl.semaphore_wait(barrier, NXD - 1 + NZD - 1 + extra)

    @pl.when((x == 0) & (z > 0))
    def _():
        for copy in crossing(True):
            copy.start()

    @pl.when((x == last_x) & (z < last_z))
    def _():
        for copy in crossing(False):
            copy.start()

    for turn in (2, 1, 3):
        copy = remote(s1.at[turn], r1.at[x], ss1.at[turn - 1], rs1.at[x], z * NXD + lax.rem(x + turn, NXD))
        copy.start()
        sends.append(copy)
    local_sums((0,))
    r1[x] = s1[0]

    for copy in down_loads:
        copy.wait()
    segments = dbuf.shape[2] // SEG
    for s in range(segments):
        for p in range(spec):
            wseg[p, s : s + 1] = wallbuf[p, pl.ds(sg[s], 1)]
    sub = lax.broadcasted_iota(jnp.int32, (segments, 128), 0)
    for r, (p, c) in enumerate(lines):
        cols = slice(c * 128, (c + 1) * 128)
        col = courbuf[p : p + 1, cols]
        factor = 1.0 / ((1.0 + col) * (1.0 + wseg[p, :, cols]))
        fac[r] = factor
        rate[r] = col * factor
    state = [jnp.zeros((segments, 128), jnp.float32) for _ in lines]
    for j in range(SEG):
        for r, (p, c) in enumerate(lines):
            state[r] = rate[r] * state[r] + fac[r] * dbuf[p, c, pl.ds(j, segments, stride=SEG), :]
    passed = [rate[r] for r in range(len(lines))]
    for _ in range(4):
        passed = [a * a for a in passed]
    for shift in (1, 2, 4):
        ok = sub >= shift
        for r in range(len(lines)):
            a_prev = jnp.where(ok, pltpu.roll(passed[r], shift, 0), 1.0)
            h_prev = jnp.where(ok, pltpu.roll(state[r], shift, 0), 0.0)
            state[r] = passed[r] * h_prev + state[r]
            passed[r] = passed[r] * a_prev
    zero_rows = jnp.zeros((d1.shape[1], 128), jnp.float32)
    for q in range(NXD):
        d1[q] = zero_rows
        d3[q] = zero_rows
    for r in range(len(lines)):
        pre_a[r] = jnp.where(sub >= 1, pltpu.roll(passed[r], 1, 0), 1.0)
        pre_h[r] = jnp.where(sub >= 1, pltpu.roll(state[r], 1, 0), 0.0)
        q, i = divmod(r, per)
        d1[q, i : i + 1] = passed[r][segments - 1 : segments]
        d1[q, per + i : per + i + 1] = state[r][segments - 1 : segments]

    for copy in small_loads:
        copy.wait()
    fires = [(fx[i] - me * XL, ht[hi[i]] * time_step) for i in range(fx.shape[0])]

    def heat_at(k):
        total = jnp.float32(0.0)
        for place, release in fires:
            total = total + jnp.where(place == k, release, 0.0)
        return total

    def transported(f, u, ahead, behind, heat):
        bend = half * u
        return ahead * (kappa_along - bend) + behind * (kappa_along + bend) + diffusivity_depth * (f + along_height(f)) + heat

    @pl.when(me == last)
    def _():
        heat = heat_at(XL - 1) * profbuf[...]
        from_lane = lax.broadcasted_iota(jnp.int32, (128, 128), 0)
        to_lane = lax.broadcasted_iota(jnp.int32, (128, 128), 1)
        pool = jnp.where(from_lane // 4 == lax.rem(to_lane, 32), 1.0 / 16.0, 0.0)
        row = lax.broadcasted_iota(jnp.int32, (rows, 128), 0)
        kept = lax.rem(row, 16) // 4 == lane // 32
        for p in range(spec):
            layer = transported(tail[p, 1], fbuf[0, XL - 1], jnp.zeros((rows, 128), jnp.float32), tail[p, 0], source_yields[p + 1] * heat)
            pooled = jnp.dot(layer, pool, precision=lax.Precision.HIGHEST, preferred_element_type=jnp.float32)
            pooled = jnp.where(kept, pooled, 0.0)
            for c in range(chunks):
                q, i = divmod(p * chunks + c, per)
                d1[q, per + i : per + i + 1] = jnp.sum(pooled[16 * c : 16 * c + 16], axis=0, keepdims=True)

    to_row(d1, e1, sd1, rd1)
    e1[x] = d1[x]

    load_rest.wait()

    def inner(members):
        def layer(k):
            heat = heat_at(k)
            u = fbuf[0, k]
            bend = half * u
            before, after = kappa_along + bend, kappa_along - bend
            shape = profbuf[...]
            for i in members:
                f = fbuf[i, k]
                moved = fbuf[i, k + 1] * after + fbuf[i, k - 1] * before + diffusivity_depth * (f + along_height(f))
                near_out[i, k] = moved + (source_yields[i] * heat) * shape

        def pair(n, carry):
            layer(2 * n + 1)
            layer(2 * n + 2)
            return carry

        lax.fori_loop(0, (XL - 2) // 2, pair, 0)

    inner((1, 2))

    @pl.when(z > 0)
    def _():
        remote(cross.at[0], cross.at[0], ssc.at[0, 0], rsc.at[0], me).wait_recv()

    @pl.when(z == 0)
    def _():
        cross[0] = jnp.zeros((quarter, 128), jnp.float32)

    @pl.when(z < last_z)
    def _():
        remote(cross.at[1], cross.at[1], ssc.at[0, 0], rsc.at[1], me).wait_recv()

    @pl.when(z == last_z)
    def _():
        cross[1] = jnp.zeros((quarter, 128), jnp.float32)

    from_row(r1, ss1, rs1)
    lows = [r1[i, 2 * quarter : 3 * quarter] for i in range(NXD)]
    highs = [r1[i, 3 * quarter : 4 * quarter] for i in range(NXD)]
    sum_f, sum_b = [], []
    for i in range(NXD):
        before = cross[0] if i == 0 else highs[i - 1]
        after = cross[1] if i == NXD - 1 else lows[i + 1]
        at_low = before * (kappa_along + half * lows[i])
        at_high = after * (kappa_along - half * highs[i])
        sum_f.append(r1[i, 0:quarter] + power(XL - 1) * at_low + at_high)
        sum_b.append(r1[i, quarter : 2 * quarter] + at_low + power(XL - 1) * at_high)
    group_f = sum_f[0]
    for i in range(1, NXD):
        group_f = power(XL) * group_f + sum_f[i]
    group_b = sum_b[NXD - 1]
    for i in reversed(range(NXD - 1)):
        group_b = power(XL) * group_b + sum_b[i]
    s2[0] = ROUND * (group_f + pick([power(GROUP + 2 + 2 * GROUP * i) for i in range(NZD)], z) * group_b)
    s2[1] = ROUND * (group_b + pick([power(GROUP * (2 * NZD - 1) - 2 * GROUP * i) for i in range(NZD)], z) * group_f)
    def to_first():
        return [
            remote(s2.at[1], r4.at[z - FAR[0], x], ss4.at[k - 1], rs4.at[z - FAR[0], x], lax.rem(x + k, NXD))
            for k in (2, 1, 3)
        ]

    @pl.when(is_far)
    def _():
        for copy in to_first():
            copy.start()

    to_column(s2, r2, ss2, rs2)

    from_row(e1, sd1, rd1)
    rates = [e1[i, 0:per] for i in range(NXD)]
    drives = [e1[i, per : 2 * per] for i in range(NXD)]
    group_a, group_h = rates[0], drives[0]
    for i in range(1, NXD):
        group_a, group_h = rates[i] * group_a, rates[i] * group_h + drives[i]
    for side in range(2):
        d2[side] = zero_rows
        d2[side, 0:per] = group_a
        d2[side, per : 2 * per] = jnp.where(z == last_z, drives[NXD - 1], group_h)
    to_column(d2, e2, sd2, rd2)
    r2[z] = s2[0]
    e2[z] = d2[0]

    up = remote(fbuf.at[:, pl.ds(XL - 1, 1)], halo.at[0], ssh.at[0], rsh.at[0], me + 1)
    low = remote(fbuf.at[:, pl.ds(0, 1)], halo.at[1], ssh.at[1], rsh.at[1], me - 1)

    @pl.when(me < last)
    def _():
        up.start()

    @pl.when(me > 0)
    def _():
        low.start()

    inner((3, 4))

    @pl.when(jnp.logical_not(early))
    def _():
        two_sided()

    def arrived(k):
        source = lax.rem(z + k, NZD)
        remote(r2.at[source], r2.at[source], ss2.at[0], rs2.at[source], me).wait_recv()

    def add_from(k):
        part = r2[lax.rem(z + k, NZD)]
        for side, (below, above) in enumerate(((from_below_f, from_above_f), (from_below_b, from_above_b))):
            values = [below(i, (i + k) % NZD) if (i + k) % NZD < i else above(i, (i + k) % NZD) for i in range(NZD)]
            total[side] = total[side] + pick(values, z) * part

    near_rows = [k for k in range(1, NZD) if k not in FAR]
    for k in near_rows:
        arrived(k)
    total[0] = ROUND * (pick([power(2 * GROUP * i + 2) for i in range(NZD)], z) * group_b + power(2 * LENGTH - GROUP + 2) * group_f)
    total[1] = ROUND * (pick([power(2 * GROUP * (NZD - 1 - i)) for i in range(NZD)], z) * group_f + power(2 * LENGTH - GROUP + 2) * group_b)
    for k in near_rows:
        add_from(k)

    @pl.when(z > 0)
    def _():
        for k in FAR:
            arrived(k)
        for k in FAR:
            add_from(k)

    in_f, in_b = total[0], total[1]
    f_at, b_at = in_f, in_b
    for i in range(NXD):
        s3[i, 0:quarter] = f_at
        f_at = power(XL) * f_at + sum_f[i]
    for i in reversed(range(NXD)):
        s3[i, quarter : 2 * quarter] = b_at
        b_at = power(XL) * b_at + sum_b[i]
    to_row(s3, r3, ss3, rs3)

    def from_row_of(k):
        source = lax.rem(z + k, NZD)
        remote(e2.at[source], e2.at[source], sd2.at[0], rd2.at[source], me).wait_recv()

    @pl.when(z > 0)
    def _():
        for k in range(1, NZD):
            from_row_of(k)

    @pl.when(z == 0)
    def _():
        from_row_of(last_z)

    carry[0:per] = e2[last_z, per : 2 * per]

    @pl.when(z > 0)
    def _():
        arrive = carry[0:per]
        for s in range(NZD - 1):
            passed_on = e2[s, 0:per] * arrive + e2[s, per : 2 * per]
            arrive = jnp.where(s < z, passed_on, arrive)
        carry[0:per] = arrive

    arrive = carry[0:per]
    for i in range(NXD):
        d3[i, 0:per] = arrive
        arrive = rates[i] * arrive + drives[i]
    to_row(d3, e3, sd3, rd3)
    r3[x] = s3[x]
    e3[x] = d3[x]

    @pl.when(me > 0)
    def _():
        remote(halo.at[0], halo.at[0], ssh.at[0], rsh.at[0], me).wait_recv()

    @pl.when(me == 0)
    def _():
        halo[0] = jnp.zeros(halo.shape[1:], jnp.float32)

    @pl.when(me < last)
    def _():
        remote(halo.at[1], halo.at[1], ssh.at[0], rsh.at[1], me).wait_recv()

    @pl.when(me == last)
    def _():
        halo[1] = jnp.zeros(halo.shape[1:], jnp.float32)

    heat_low = heat_at(0) * profbuf[...]
    heat_high = heat_at(XL - 1) * profbuf[...]
    for i in range(1, 5):
        near_out[i, 0] = transported(fbuf[i, 0], fbuf[0, 0], fbuf[i, 1], halo[0, i, 0], source_yields[i] * heat_low)
        near_out[i, XL - 1] = transported(fbuf[i, XL - 1], fbuf[0, XL - 1], halo[1, i, 0], fbuf[i, XL - 2], source_yields[i] * heat_high)

    from_row(r3, ss3, rs3)
    from_low = jnp.concatenate([r3[q, 0:quarter] for q in range(NXD)], axis=0)
    from_high = jnp.concatenate([r3[q, quarter : 2 * quarter] for q in range(NXD)], axis=0)
    edges[0] = GAIN * (ROOT * from_low + halo[0, 0, 0] * (kappa_along + half * fbuf[0, 0]))
    edges[1] = GAIN * (ROOT * from_high + halo[1, 0, 0] * (kappa_along - half * fbuf[0, XL - 1]))

    @pl.when(z == 0)
    def _():
        for k in range(1, last_z):
            from_row_of(k)
        for far in FAR:
            arrived(far)
            for k in (1, 2, 3):
                source = lax.rem(x + k, NXD)
                remote(r4.at[far - FAR[0], source], r4.at[far - FAR[0], source], ss4.at[0], rs4.at[far - FAR[0], source], me).wait_recv()
            r4[far - FAR[0], x] = r2[far]
        along = pick([power(XL * i) for i in range(NXD)], x)
        against = pick([power(XL * (NXD - 1 - i)) for i in range(NXD)], x)
        for q in range(NXD):
            part = slice(q * quarter, (q + 1) * quarter)
            up_sum = from_above_f(0, FAR[0]) * r4[0, q]
            down_sum = from_above_b(0, FAR[0]) * r4[0, q]
            for far in FAR[1:]:
                up_sum = up_sum + from_above_f(0, far) * r4[far - FAR[0], q]
                down_sum = down_sum + from_above_b(0, far) * r4[far - FAR[0], q]
            edges[0, part] = edges[0, part] + (GAIN * ROOT) * along * up_sum
            edges[1, part] = edges[1, part] + (GAIN * ROOT) * against * down_sum

    from_row(e3, sd3, rd3)
    for r in range(len(lines)):
        q, i = divmod(r, per)
        start[r] = pre_a[r] * e3[q, i : i + 1] + pre_h[r]

    for copy in sends:
        copy.wait_send()

    @pl.when(is_far)
    def _():
        for copy in to_first():
            copy.wait_send()

    @pl.when((x == 0) & (z > 0))
    def _():
        for copy in crossing(True):
            copy.wait_send()

    @pl.when((x == last_x) & (z < last_z))
    def _():
        for copy in crossing(False):
            copy.wait_send()

    @pl.when(me < last)
    def _():
        up.wait_send()

    @pl.when(me > 0)
    def _():
        low.wait_send()


def write_kernel(near_in, edges, dbuf, fac, rate, start, near_out, down_out, velocity, dnext, sem):
    copies = [
        pltpu.make_async_copy(near_in.at[i, pl.ds(h * 16, 16)], near_out.at[i, pl.ds(h * 16, 16)], sem.at[2 * i + h])
        for i in range(1, 5) for h in range(2)
    ]
    for copy in copies:
        copy.start()
    spec, chunks = dbuf.shape[:2]
    segments = dbuf.shape[2] // SEG
    for c in range(chunks):
        state = [start[p * chunks + c] for p in range(spec)]
        for j in range(SEG):
            at = pl.ds(j, segments, stride=SEG)
            for p in range(spec):
                r = p * chunks + c
                state[p] = rate[r] * state[p] + fac[r] * dbuf[p, c, at, :]
                dnext[p, c, at, :] = state[p]
        copy = pltpu.make_async_copy(dnext.at[:, c], down_out.at[:, :, pl.ds(128 * c, 128)], sem.at[10 + c])
        copy.start()
        copies.append(copy)
    for part in range(2):
        for k in range(16 * part, 16 * part + 16):
            velocity[k] = near_in[0, k] + (power(k) * edges[0] + power(XL - 1 - k) * edges[1])
        copy = pltpu.make_async_copy(velocity.at[pl.ds(16 * part, 16)], near_out.at[0, pl.ds(16 * part, 16)], sem.at[part])
        copy.start()
        copies.append(copy)
    for copy in copies:
        copy.wait()


def body(fields, down_state, fire_x, hrr_index, hrr_table, profile, courant, wall_loss, seg_table):
    f32 = jnp.float32
    rows = fields.shape[2]
    quarter = rows // NXD
    spec, cells, columns = down_state.shape
    segments = cells // SEG
    lines = spec * columns // 128
    per = lines // NXD

    small = -(-2 * per // 8) * 8
    vmem, smem, dma = pltpu.VMEM, pltpu.SMEM, pltpu.SemaphoreType.DMA
    hbm = pl.BlockSpec(memory_space=pltpu.HBM)
    in_vmem = pl.BlockSpec(memory_space=pltpu.VMEM)
    chunked = (spec, columns // 128, cells, 128)
    shapes = (fields.shape, (2, rows, 128), chunked) + ((lines, segments, 128),) * 3
    middle = pl.pallas_call(
        tunnel_kernel,
        out_shape=tuple(jax.ShapeDtypeStruct(shape, f32) for shape in shapes),
        in_specs=[hbm] * 9,
        out_specs=(in_vmem,) * len(shapes),
        scratch_shapes=[
            vmem(fields.shape, f32),
            vmem(fields.shape[1:], f32),
            vmem((2, 5, 1, rows, 128), f32),
            vmem((spec, 2, rows, 128), f32),
            vmem((spec, wall_loss.shape[0], columns), f32),
            vmem(courant.shape, f32),
            vmem(profile.shape, f32),
            vmem((NXD, 4 * quarter, 128), f32),
            vmem((NXD, 4 * quarter, 128), f32),
            vmem((2, quarter, 128), f32),
            vmem((2, quarter, 128), f32),
            vmem((NZD, quarter, 128), f32),
            vmem((NXD, 2 * quarter, 128), f32),
            vmem((NXD, 2 * quarter, 128), f32),
            vmem((len(FAR), NXD, quarter, 128), f32),
            vmem((2, quarter, 128), f32),
            vmem((small, 128), f32),
            vmem((NXD, small, 128), f32),
            vmem((NXD, small, 128), f32),
            vmem((2, small, 128), f32),
            vmem((NZD, small, 128), f32),
            vmem((NXD, small, 128), f32),
            vmem((NXD, small, 128), f32),
            vmem((spec, segments, columns), f32),
            vmem((lines, segments, 128), f32),
            vmem((lines, segments, 128), f32),
            smem(fire_x.shape, jnp.int32),
            smem(hrr_index.shape, jnp.int32),
            smem(hrr_table.shape, f32),
            smem(seg_table.shape, jnp.int32),
            dma((15,)),
            dma((NXD - 1,)),
            dma((NXD,)),
            dma((2, NXD)),
            dma((2,)),
            dma((2,)),
            dma((2,)),
            dma((NZD - 1,)),
            dma((NZD,)),
            dma((NXD - 1,)),
            dma((NXD,)),
            dma((NXD - 1,)),
            dma((len(FAR), NXD)),
            dma((NXD - 1,)),
            dma((NXD,)),
            dma((NZD - 1,)),
            dma((NZD,)),
            dma((NXD - 1,)),
            dma((NXD,)),
        ],
        compiler_params=pltpu.CompilerParams(
            collective_id=0, has_side_effects=True, vmem_limit_bytes=32 * 1024 * 1024
        ),
        name="tunnel_step",
    )(*(pltpu.with_memory_space_constraint(a, pltpu.HBM) for a in (fields, down_state, fire_x, hrr_index, hrr_table, profile, courant, jnp.transpose(wall_loss, (1, 0, 2)), seg_table)))
    return pl.pallas_call(
        write_kernel,
        out_shape=(jax.ShapeDtypeStruct(fields.shape, f32), jax.ShapeDtypeStruct(down_state.shape, f32)),
        in_specs=[in_vmem] * len(shapes),
        out_specs=(hbm, hbm),
        scratch_shapes=[vmem(fields.shape[1:], f32), vmem(chunked, f32), dma((14,))],
        compiler_params=pltpu.CompilerParams(vmem_limit_bytes=16 * 1024 * 1024),
        name="write_out",
    )(*middle)


def solution(mesh):
    placed = (
        P("scen", "near", "sect", None),
        P("scen", "near", "sect"),
        P("scen"),
        P("scen"),
        P(),
        P("sect", None),
        P(None, "sect"),
        P(None, None, "sect"),
        P("near"),
    )
    return jax.shard_map(
        body,
        mesh=mesh,
        in_specs=placed,
        out_specs=(P("scen", "near", "sect", None), P("scen", "near", "sect")),
        check_vma=False,
    )
```

```python
import math

import jax
import jax.numpy as jnp
from jax import lax
from jax.experimental import pallas as pl
from jax.experimental.pallas import tpu as pltpu
from jax.sharding import PartitionSpec as P

MESH = pl.DeviceIdType.MESH

SEG = 16
time_step = 0.1
kappa_along = 0.2
diffusivity_depth = 0.2
buoyancy = 0.5
screening = 0.0003
source_yields = (0.0, 1.0, 0.5, 0.2, -0.3)

XL = 32
NXD = 4
NZD = 8
LENGTH = XL * NXD * NZD

_t = 2.0 + screening
ROOT = (_t - math.sqrt(_t * _t - 4.0)) / 2.0
GAIN = screening / (1.0 / ROOT - ROOT)


def power(n):
    return ROOT**n


ROUND = 1.0 / (1.0 - power(2 * LENGTH + 2))
GROUP = XL * NXD

FAR = (4, 5)
FIRST = 1


def pick(values, index):
    chosen = jnp.float32(values[0])
    for i in range(1, len(values)):
        chosen = jnp.where(index == i, jnp.float32(values[i]), chosen)
    return chosen


def from_below_f(z, s):
    return power(GROUP * (z - 1 - s))


def from_below_b(z, s):
    return power(GROUP * (2 * NZD - 2 - z - s))


def from_above_f(z, s):
    return power(GROUP * (z + s) + 2)


def from_above_b(z, s):
    return power(GROUP * (s - z - 1))


def tunnel_kernel(
    fields, down, fire_x, hrr_index, hrr_table, profile, courant, wall, seg,
    near_out, edges, dbuf, fac, rate, start,
    fbuf, ubuf, halo, tail, wallbuf, courbuf, profbuf,
    s1, r1, cross, s2, r2, s3, r3, r4, total, carry, d1, e1, d2, e2, d3, e3, wseg, pre_a, pre_h,
    fx, hi, ht, sg,
    load_sem, ss1, rs1, ssc, rsc, ssh, rsh, ss2, rs2, ss3, rs3, ss4, rs4, sd1, rd1, sd2, rd2, sd3, rd3,
):
    velocity_loads = [pltpu.make_async_copy(fields.at[f], fbuf.at[f], load_sem.at[f]) for f in range(2)]
    for copy in velocity_loads:
        copy.start()
    me = lax.axis_index("near")
    z = me // NXD
    x = lax.rem(me, NXD)
    last, last_z, last_x = NXD * NZD - 1, NZD - 1, NXD - 1
    rows = fbuf.shape[2]
    quarter = rows // NXD
    spec = dbuf.shape[0]
    chunks = dbuf.shape[1]
    per = spec * chunks // NXD
    lines = [divmod(r, chunks) for r in range(spec * chunks)]

    def remote(src, dst, send, recv, target):
        return pltpu.make_async_remote_copy(
            src_ref=src, dst_ref=dst, send_sem=send, recv_sem=recv,
            device_id={"near": target}, device_id_type=MESH,
        )

    barrier = pltpu.get_barrier_semaphore()

    def greet(target):
        pl.semaphore_signal(barrier, inc=1, device_id={"near": target}, device_id_type=MESH)

    for k in (4, 3, 5, 2, 6, 1, 7):
        greet(lax.rem(z + k, NZD) * NXD + x)
    for k in (2, 1, 3):
        greet(z * NXD + lax.rem(x + k, NXD))

    @pl.when(z < FIRST)
    def _():
        for k in (1, 2, 3):
            for far in FAR:
                greet((z + far) * NXD + lax.rem(x + k, NXD))

    far_pairs = [(t, i) for t in range(FIRST) for i in range(len(FAR))]

    @pl.when(z < last_z)
    def _():
        greet((z + 1) * NXD)

    @pl.when(z > 0)
    def _():
        greet((z - 1) * NXD + last_x)

    loads = [
        pltpu.make_async_copy(src, dst, load_sem.at[2 + i])
        for i, (src, dst) in enumerate((
            (seg, sg),
            (courant, courbuf),
            (wall, wallbuf),
        ) + tuple((down.at[:, :, pl.ds(128 * c, 128)], dbuf.at[:, c]) for c in range(chunks)) + (
            (fire_x, fx),
            (hrr_index, hi),
            (hrr_table, ht),
            (profile, profbuf),
            (fields.at[pl.ds(1, spec), pl.ds(XL - 2, 2)], tail),
            (fields.at[pl.ds(2, 3)], fbuf.at[pl.ds(2, 3)]),
        ))
    ]
    for copy in loads:
        copy.start()
    down_loads, small_loads, load_rest = loads[:-6], loads[-6:-1], loads[-1]

    lane = lax.broadcasted_iota(jnp.int32, (rows, 128), 1)
    not_first = lane > 0
    not_last = lane < 127

    def along_height(f):
        return jnp.where(not_first, pltpu.roll(f, 1, 1), 0.0) + jnp.where(not_last, pltpu.roll(f, 127, 1), 0.0)

    half = 0.5 * time_step
    keep = 1.0 - 2.0 * kappa_along - 2.0 * diffusivity_depth
    def velocity(k, ahead, behind):
        u = fbuf[0, k]
        bend = half * u
        star = (time_step * buoyancy) * fbuf[1, k] + diffusivity_depth * (u + along_height(u))
        if ahead is not None:
            star = star + ahead * (kappa_along - bend)
        if behind is not None:
            star = star + behind * (kappa_along + bend)
        return star

    def two_sided():
        star = velocity(0, fbuf[0, 1], None)
        ubuf[0] = star
        near_out[0, 0] = star

        def forward(n, f):
            for k in (2 * n + 1, 2 * n + 2):
                star = velocity(k, fbuf[0, k + 1], fbuf[0, k - 1])
                f = ROOT * f + star
                ubuf[k] = star
                near_out[0, k] = f
            return f

        f = lax.fori_loop(0, (XL - 2) // 2, forward, star)
        star = velocity(XL - 1, None, fbuf[0, XL - 2])
        ubuf[XL - 1] = star
        near_out[0, XL - 1] = ROOT * f + star

        def backward(n, b):
            for k in (XL - 1 - 2 * n, XL - 2 - 2 * n):
                near_out[0, k] = GAIN * (near_out[0, k] + ROOT * b)
                b = ubuf[k] + ROOT * b
            return b

        lax.fori_loop(0, XL // 2, backward, jnp.zeros((rows, 128), jnp.float32))

    early = z < NZD // 2
    for copy in velocity_loads:
        copy.wait()

    @pl.when(early)
    def _():
        two_sided()

    sends = []

    def to_row(out, into, send, recv):
        for k in (2, 1, 3):
            to = lax.rem(x + k, NXD)
            copy = remote(out.at[to], into.at[x], send.at[k - 1], recv.at[x], z * NXD + to)
            copy.start()
            sends.append(copy)

    def from_row(into, send, recv):
        for k in range(1, NXD):
            source = lax.rem(x + k, NXD)
            remote(into.at[source], into.at[source], send.at[0], recv.at[source], me).wait_recv()

    def to_column(out, into, send, recv):
        for k in (4, 3, 5, 2, 6, 1, 7):
            to = lax.rem(z + k, NZD)
            copy = remote(out.at[jnp.where(to > z, 0, 1)], into.at[z], send.at[k - 1], recv.at[z], to * NXD + x)
            copy.start()
            sends.append(copy)

    def from_column(into, send, recv):
        for k in range(1, NZD):
            source = lax.rem(z + k, NZD)
            remote(into.at[source], into.at[source], send.at[0], recv.at[source], me).wait_recv()

    def crossing(low):
        target = (z - 1 if low else z + 1) * NXD
        return [
            remote(s1.at[k, pl.ds((2 if low else 3) * quarter, quarter)], cross.at[1 if low else 0],
                   ssc.at[0 if low else 1, k], rsc.at[1 if low else 0], target + lax.rem(x + k, NXD))
            for k in range(NXD)
        ]

    def columns(turn):
        return pl.ds(pl.multiple_of(lax.rem(x + turn, NXD) * quarter, quarter), quarter)

    for turn in range(NXD):
        s1[turn, 2 * quarter : 3 * quarter] = fbuf[0, 0, columns(turn)]
        s1[turn, 3 * quarter : 4 * quarter] = fbuf[0, XL - 1, columns(turn)]

    inside = lax.broadcasted_iota(jnp.int32, (quarter, 128), 1)

    def local_sums(turns):
        here = {t: fbuf[0, 0, columns(t)] for t in turns}
        behind, total = {}, {}
        for k in range(XL):
            for t in turns:
                ahead = fbuf[0, k + 1, columns(t)] if k < XL - 1 else None
                bent = fbuf[1, k, columns(t)]
                if k == 0:
                    bent = bent - here[t] * ahead
                    total[t] = (here[t], bent, here[t], bent)
                else:
                    bent = bent + here[t] * (behind[t] if ahead is None else behind[t] - ahead)
                    up_u, up_b, down_u, down_b = total[t]
                    total[t] = (ROOT * up_u + here[t], ROOT * up_b + bent, down_u + power(k) * here[t], down_b + power(k) * bent)
                behind[t], here[t] = here[t], ahead
        for t in turns:
            up_u, up_b, down_u, down_b = total[t]
            first, final = fbuf[0, 0, columns(t)], behind[t]
            ends = (
                (up_u, up_b, ROOT * (up_u - power(XL - 1) * first) + (1.0 / ROOT) * (up_u - final)),
                (down_u, down_b, (1.0 / ROOT) * (down_u - first) + ROOT * (down_u - power(XL - 1) * final)),
            )
            for side, (plain, bent, shifted) in enumerate(ends):
                high = jnp.where(inside > 0, pltpu.roll(plain, 1, 1), 0.0) + jnp.where(inside < 127, pltpu.roll(plain, 127, 1), 0.0)
                s1[t, side * quarter : (side + 1) * quarter] = half * bent + keep * plain + kappa_along * shifted + diffusivity_depth * high

    local_sums((2, 1, 3))
    extra = 4 * jnp.where((x == 0) & (z > 0), 1, 0) + 4 * jnp.where((x == last_x) & (z < last_z), 1, 0)
    for t, i in far_pairs:
        extra = extra + (NXD - 1) * jnp.where(z == t + FAR[i], 1, 0)
    pl.semaphore_wait(barrier, NXD - 1 + NZD - 1 + extra)

    @pl.when((x == 0) & (z > 0))
    def _():
        for copy in crossing(True):
            copy.start()

    @pl.when((x == last_x) & (z < last_z))
    def _():
        for copy in crossing(False):
            copy.start()

    for turn in (2, 1, 3):
        copy = remote(s1.at[turn], r1.at[x], ss1.at[turn - 1], rs1.at[x], z * NXD + lax.rem(x + turn, NXD))
        copy.start()
        sends.append(copy)
    local_sums((0,))
    r1[x] = s1[0]

    for copy in down_loads:
        copy.wait()
    segments = dbuf.shape[2] // SEG
    for s in range(segments):
        for p in range(spec):
            wseg[p, s : s + 1] = wallbuf[p, pl.ds(sg[s], 1)]
    sub = lax.broadcasted_iota(jnp.int32, (segments, 128), 0)
    for r, (p, c) in enumerate(lines):
        cols = slice(c * 128, (c + 1) * 128)
        col = courbuf[p : p + 1, cols]
        factor = 1.0 / ((1.0 + col) * (1.0 + wseg[p, :, cols]))
        fac[r] = factor
        rate[r] = col * factor
    state = [jnp.zeros((segments, 128), jnp.float32) for _ in lines]
    for j in range(SEG):
        for r, (p, c) in enumerate(lines):
            state[r] = rate[r] * state[r] + fac[r] * dbuf[p, c, pl.ds(j, segments, stride=SEG), :]
    passed = [rate[r] for r in range(len(lines))]
    for _ in range(4):
        passed = [a * a for a in passed]
    for shift in (1, 2, 4):
        ok = sub >= shift
        for r in range(len(lines)):
            a_prev = jnp.where(ok, pltpu.roll(passed[r], shift, 0), 1.0)
            h_prev = jnp.where(ok, pltpu.roll(state[r], shift, 0), 0.0)
            state[r] = passed[r] * h_prev + state[r]
            passed[r] = passed[r] * a_prev
    zero_rows = jnp.zeros((d1.shape[1], 128), jnp.float32)
    for q in range(NXD):
        d1[q] = zero_rows
        d3[q] = zero_rows
    for r in range(len(lines)):
        pre_a[r] = jnp.where(sub >= 1, pltpu.roll(passed[r], 1, 0), 1.0)
        pre_h[r] = jnp.where(sub >= 1, pltpu.roll(state[r], 1, 0), 0.0)
        q, i = divmod(r, per)
        d1[q, i : i + 1] = passed[r][segments - 1 : segments]
        d1[q, per + i : per + i + 1] = state[r][segments - 1 : segments]

    for copy in small_loads:
        copy.wait()
    fires = [(fx[i] - me * XL, ht[hi[i]] * time_step) for i in range(fx.shape[0])]

    def heat_at(k):
        total = jnp.float32(0.0)
        for place, release in fires:
            total = total + jnp.where(place == k, release, 0.0)
        return total

    def transported(f, u, ahead, behind, heat):
        bend = half * u
        return ahead * (kappa_along - bend) + behind * (kappa_along + bend) + diffusivity_depth * (f + along_height(f)) + heat

    @pl.when(me == last)
    def _():
        heat = heat_at(XL - 1) * profbuf[...]
        from_lane = lax.broadcasted_iota(jnp.int32, (128, 128), 0)
        to_lane = lax.broadcasted_iota(jnp.int32, (128, 128), 1)
        pool = jnp.where(from_lane // 4 == lax.rem(to_lane, 32), 1.0 / 16.0, 0.0)
        row = lax.broadcasted_iota(jnp.int32, (rows, 128), 0)
        kept = lax.rem(row, 16) // 4 == lane // 32
        for p in range(spec):
            layer = transported(tail[p, 1], fbuf[0, XL - 1], jnp.zeros((rows, 128), jnp.float32), tail[p, 0], source_yields[p + 1] * heat)
            pooled = jnp.dot(layer, pool, precision=lax.Precision.HIGHEST, preferred_element_type=jnp.float32)
            pooled = jnp.where(kept, pooled, 0.0)
            for c in range(chunks):
                q, i = divmod(p * chunks + c, per)
                d1[q, per + i : per + i + 1] = jnp.sum(pooled[16 * c : 16 * c + 16], axis=0, keepdims=True)

    to_row(d1, e1, sd1, rd1)
    e1[x] = d1[x]

    load_rest.wait()

    def inner(members):
        def layer(k):
            heat = heat_at(k)
            u = fbuf[0, k]
            bend = half * u
            before, after = kappa_along + bend, kappa_along - bend
            shape = profbuf[...]
            for i in members:
                f = fbuf[i, k]
                moved = fbuf[i, k + 1] * after + fbuf[i, k - 1] * before + diffusivity_depth * (f + along_height(f))
                near_out[i, k] = moved + (source_yields[i] * heat) * shape

        def pair(n, carry):
            layer(2 * n + 1)
            layer(2 * n + 2)
            return carry

        lax.fori_loop(0, (XL - 2) // 2, pair, 0)

    inner((1, 2))

    @pl.when(z > 0)
    def _():
        remote(cross.at[0], cross.at[0], ssc.at[0, 0], rsc.at[0], me).wait_recv()

    @pl.when(z == 0)
    def _():
        cross[0] = jnp.zeros((quarter, 128), jnp.float32)

    @pl.when(z < last_z)
    def _():
        remote(cross.at[1], cross.at[1], ssc.at[0, 0], rsc.at[1], me).wait_recv()

    @pl.when(z == last_z)
    def _():
        cross[1] = jnp.zeros((quarter, 128), jnp.float32)

    from_row(r1, ss1, rs1)
    lows = [r1[i, 2 * quarter : 3 * quarter] for i in range(NXD)]
    highs = [r1[i, 3 * quarter : 4 * quarter] for i in range(NXD)]
    sum_f, sum_b = [], []
    for i in range(NXD):
        before = cross[0] if i == 0 else highs[i - 1]
        after = cross[1] if i == NXD - 1 else lows[i + 1]
        at_low = before * (kappa_along + half * lows[i])
        at_high = after * (kappa_along - half * highs[i])
        sum_f.append(r1[i, 0:quarter] + power(XL - 1) * at_low + at_high)
        sum_b.append(r1[i, quarter : 2 * quarter] + at_low + power(XL - 1) * at_high)
    group_f = sum_f[0]
    for i in range(1, NXD):
        group_f = power(XL) * group_f + sum_f[i]
    group_b = sum_b[NXD - 1]
    for i in reversed(range(NXD - 1)):
        group_b = power(XL) * group_b + sum_b[i]
    s2[0] = ROUND * (group_f + pick([power(GROUP + 2 + 2 * GROUP * i) for i in range(NZD)], z) * group_b)
    s2[1] = ROUND * (group_b + pick([power(GROUP * (2 * NZD - 1) - 2 * GROUP * i) for i in range(NZD)], z) * group_f)
    def to_first(t, i):
        return [
            remote(s2.at[1], r4.at[i, x], ss4.at[i, k - 1], rs4.at[i, x], t * NXD + lax.rem(x + k, NXD))
            for k in (2, 1, 3)
        ]

    for t, i in far_pairs:

        @pl.when(z == t + FAR[i])
        def _():
            for copy in to_first(t, i):
                copy.start()

    to_column(s2, r2, ss2, rs2)

    from_row(e1, sd1, rd1)
    rates = [e1[i, 0:per] for i in range(NXD)]
    drives = [e1[i, per : 2 * per] for i in range(NXD)]
    group_a, group_h = rates[0], drives[0]
    for i in range(1, NXD):
        group_a, group_h = rates[i] * group_a, rates[i] * group_h + drives[i]
    for side in range(2):
        d2[side] = zero_rows
        d2[side, 0:per] = group_a
        d2[side, per : 2 * per] = jnp.where(z == last_z, drives[NXD - 1], group_h)
    to_column(d2, e2, sd2, rd2)
    r2[z] = s2[0]
    e2[z] = d2[0]

    up = remote(fbuf.at[:, pl.ds(XL - 1, 1)], halo.at[0], ssh.at[0], rsh.at[0], me + 1)
    low = remote(fbuf.at[:, pl.ds(0, 1)], halo.at[1], ssh.at[1], rsh.at[1], me - 1)

    @pl.when(me < last)
    def _():
        up.start()

    @pl.when(me > 0)
    def _():
        low.start()

    inner((3, 4))

    @pl.when(jnp.logical_not(early))
    def _():
        two_sided()

    def arrived(k):
        source = lax.rem(z + k, NZD)
        remote(r2.at[source], r2.at[source], ss2.at[0], rs2.at[source], me).wait_recv()

    def add_from(k):
        part = r2[lax.rem(z + k, NZD)]
        for side, (below, above) in enumerate(((from_below_f, from_above_f), (from_below_b, from_above_b))):
            values = [below(i, (i + k) % NZD) if (i + k) % NZD < i else above(i, (i + k) % NZD) for i in range(NZD)]
            total[side] = total[side] + pick(values, z) * part

    near_rows = [k for k in range(1, NZD) if k not in FAR]
    for k in near_rows:
        arrived(k)
    total[0] = ROUND * (pick([power(2 * GROUP * i + 2) for i in range(NZD)], z) * group_b + power(2 * LENGTH - GROUP + 2) * group_f)
    total[1] = ROUND * (pick([power(2 * GROUP * (NZD - 1 - i)) for i in range(NZD)], z) * group_f + power(2 * LENGTH - GROUP + 2) * group_b)
    for k in near_rows:
        add_from(k)

    @pl.when(z >= FIRST)
    def _():
        for k in FAR:
            arrived(k)
        for k in FAR:
            add_from(k)

    in_f, in_b = total[0], total[1]
    f_at, b_at = in_f, in_b
    for i in range(NXD):
        s3[i, 0:quarter] = f_at
        f_at = power(XL) * f_at + sum_f[i]
    for i in reversed(range(NXD)):
        s3[i, quarter : 2 * quarter] = b_at
        b_at = power(XL) * b_at + sum_b[i]
    to_row(s3, r3, ss3, rs3)

    def from_row_at(k, needed):
        source = lax.rem(z + k, NZD)
        uses = (source < z) | (source == last_z)

        @pl.when(uses if needed else jnp.logical_not(uses))
        def _():
            remote(e2.at[source], e2.at[source], sd2.at[0], rd2.at[source], me).wait_recv()

    for k in range(1, NZD):
        from_row_at(k, True)
    carry[0:per] = e2[last_z, per : 2 * per]
    for s in range(NZD - 1):

        @pl.when(s < z)
        def _():
            carry[0:per] = e2[s, 0:per] * carry[0:per] + e2[s, per : 2 * per]

    arrive = carry[0:per]
    for i in range(NXD):
        d3[i, 0:per] = arrive
        arrive = rates[i] * arrive + drives[i]
    to_row(d3, e3, sd3, rd3)
    r3[x] = s3[x]
    e3[x] = d3[x]

    @pl.when(me > 0)
    def _():
        remote(halo.at[0], halo.at[0], ssh.at[0], rsh.at[0], me).wait_recv()

    @pl.when(me == 0)
    def _():
        halo[0] = jnp.zeros(halo.shape[1:], jnp.float32)

    @pl.when(me < last)
    def _():
        remote(halo.at[1], halo.at[1], ssh.at[0], rsh.at[1], me).wait_recv()

    @pl.when(me == last)
    def _():
        halo[1] = jnp.zeros(halo.shape[1:], jnp.float32)

    heat_low = heat_at(0) * profbuf[...]
    heat_high = heat_at(XL - 1) * profbuf[...]
    for i in range(1, 5):
        near_out[i, 0] = transported(fbuf[i, 0], fbuf[0, 0], fbuf[i, 1], halo[0, i, 0], source_yields[i] * heat_low)
        near_out[i, XL - 1] = transported(fbuf[i, XL - 1], fbuf[0, XL - 1], halo[1, i, 0], fbuf[i, XL - 2], source_yields[i] * heat_high)

    from_row(r3, ss3, rs3)
    from_low = jnp.concatenate([r3[q, 0:quarter] for q in range(NXD)], axis=0)
    from_high = jnp.concatenate([r3[q, quarter : 2 * quarter] for q in range(NXD)], axis=0)
    edges[0] = GAIN * (ROOT * from_low + halo[0, 0, 0] * (kappa_along + half * fbuf[0, 0]))
    edges[1] = GAIN * (ROOT * from_high + halo[1, 0, 0] * (kappa_along - half * fbuf[0, XL - 1]))

    for k in range(1, NZD):
        from_row_at(k, False)

    @pl.when(z < FIRST)
    def _():
        for i, far in enumerate(FAR):
            arrived(far)
            for k in (1, 2, 3):
                source = lax.rem(x + k, NXD)
                remote(r4.at[i, source], r4.at[i, source], ss4.at[0, 0], rs4.at[i, source], me).wait_recv()
            r4[i, x] = r2[lax.rem(z + far, NZD)]
        along = pick([power(XL * i) for i in range(NXD)], x)
        against = pick([power(XL * (NXD - 1 - i)) for i in range(NXD)], x)
        for q in range(NXD):
            part = slice(q * quarter, (q + 1) * quarter)
            up_sum, down_sum = jnp.zeros((quarter, 128), jnp.float32), jnp.zeros((quarter, 128), jnp.float32)
            for i, far in enumerate(FAR):
                up_sum = up_sum + pick([from_above_f(t, t + far) for t in range(FIRST)], z) * r4[i, q]
                down_sum = down_sum + pick([from_above_b(t, t + far) for t in range(FIRST)], z) * r4[i, q]
            edges[0, part] = edges[0, part] + (GAIN * ROOT) * along * up_sum
            edges[1, part] = edges[1, part] + (GAIN * ROOT) * against * down_sum

    from_row(e3, sd3, rd3)
    for r in range(len(lines)):
        q, i = divmod(r, per)
        start[r] = pre_a[r] * e3[q, i : i + 1] + pre_h[r]

    for copy in sends:
        copy.wait_send()

    for t, i in far_pairs:

        @pl.when(z == t + FAR[i])
        def _():
            for copy in to_first(t, i):
                copy.wait_send()

    @pl.when((x == 0) & (z > 0))
    def _():
        for copy in crossing(True):
            copy.wait_send()

    @pl.when((x == last_x) & (z < last_z))
    def _():
        for copy in crossing(False):
            copy.wait_send()

    @pl.when(me < last)
    def _():
        up.wait_send()

    @pl.when(me > 0)
    def _():
        low.wait_send()


def write_kernel(near_in, edges, dbuf, fac, rate, start, near_out, down_out, velocity, dnext, sem):
    copies = [
        pltpu.make_async_copy(near_in.at[i, pl.ds(h * 16, 16)], near_out.at[i, pl.ds(h * 16, 16)], sem.at[2 * i + h])
        for i in range(1, 5) for h in range(2)
    ]
    for copy in copies:
        copy.start()
    spec, chunks = dbuf.shape[:2]
    segments = dbuf.shape[2] // SEG
    for c in range(chunks):
        state = [start[p * chunks + c] for p in range(spec)]
        for j in range(SEG):
            at = pl.ds(j, segments, stride=SEG)
            for p in range(spec):
                r = p * chunks + c
                state[p] = rate[r] * state[p] + fac[r] * dbuf[p, c, at, :]
                dnext[p, c, at, :] = state[p]
        copy = pltpu.make_async_copy(dnext.at[:, c], down_out.at[:, :, pl.ds(128 * c, 128)], sem.at[10 + c])
        copy.start()
        copies.append(copy)
    for part in range(2):
        for k in range(16 * part, 16 * part + 16):
            velocity[k] = near_in[0, k] + (power(k) * edges[0] + power(XL - 1 - k) * edges[1])
        copy = pltpu.make_async_copy(velocity.at[pl.ds(16 * part, 16)], near_out.at[0, pl.ds(16 * part, 16)], sem.at[part])
        copy.start()
        copies.append(copy)
    for copy in copies:
        copy.wait()


def body(fields, down_state, fire_x, hrr_index, hrr_table, profile, courant, wall_loss, seg_table):
    f32 = jnp.float32
    rows = fields.shape[2]
    quarter = rows // NXD
    spec, cells, columns = down_state.shape
    segments = cells // SEG
    lines = spec * columns // 128
    per = lines // NXD

    small = -(-2 * per // 8) * 8
    vmem, smem, dma = pltpu.VMEM, pltpu.SMEM, pltpu.SemaphoreType.DMA
    hbm = pl.BlockSpec(memory_space=pltpu.HBM)
    in_vmem = pl.BlockSpec(memory_space=pltpu.VMEM)
    chunked = (spec, columns // 128, cells, 128)
    shapes = (fields.shape, (2, rows, 128), chunked) + ((lines, segments, 128),) * 3
    middle = pl.pallas_call(
        tunnel_kernel,
        out_shape=tuple(jax.ShapeDtypeStruct(shape, f32) for shape in shapes),
        in_specs=[hbm] * 9,
        out_specs=(in_vmem,) * len(shapes),
        scratch_shapes=[
            vmem(fields.shape, f32),
            vmem(fields.shape[1:], f32),
            vmem((2, 5, 1, rows, 128), f32),
            vmem((spec, 2, rows, 128), f32),
            vmem((spec, wall_loss.shape[0], columns), f32),
            vmem(courant.shape, f32),
            vmem(profile.shape, f32),
            vmem((NXD, 4 * quarter, 128), f32),
            vmem((NXD, 4 * quarter, 128), f32),
            vmem((2, quarter, 128), f32),
            vmem((2, quarter, 128), f32),
            vmem((NZD, quarter, 128), f32),
            vmem((NXD, 2 * quarter, 128), f32),
            vmem((NXD, 2 * quarter, 128), f32),
            vmem((len(FAR), NXD, quarter, 128), f32),
            vmem((2, quarter, 128), f32),
            vmem((small, 128), f32),
            vmem((NXD, small, 128), f32),
            vmem((NXD, small, 128), f32),
            vmem((2, small, 128), f32),
            vmem((NZD, small, 128), f32),
            vmem((NXD, small, 128), f32),
            vmem((NXD, small, 128), f32),
            vmem((spec, segments, columns), f32),
            vmem((lines, segments, 128), f32),
            vmem((lines, segments, 128), f32),
            smem(fire_x.shape, jnp.int32),
            smem(hrr_index.shape, jnp.int32),
            smem(hrr_table.shape, f32),
            smem(seg_table.shape, jnp.int32),
            dma((15,)),
            dma((NXD - 1,)),
            dma((NXD,)),
            dma((2, NXD)),
            dma((2,)),
            dma((2,)),
            dma((2,)),
            dma((NZD - 1,)),
            dma((NZD,)),
            dma((NXD - 1,)),
            dma((NXD,)),
            dma((len(FAR), NXD - 1)),
            dma((len(FAR), NXD)),
            dma((NXD - 1,)),
            dma((NXD,)),
            dma((NZD - 1,)),
            dma((NZD,)),
            dma((NXD - 1,)),
            dma((NXD,)),
        ],
        compiler_params=pltpu.CompilerParams(
            collective_id=0, has_side_effects=True, vmem_limit_bytes=32 * 1024 * 1024
        ),
        name="tunnel_step",
    )(*(pltpu.with_memory_space_constraint(a, pltpu.HBM) for a in (fields, down_state, fire_x, hrr_index, hrr_table, profile, courant, jnp.transpose(wall_loss, (1, 0, 2)), seg_table)))
    return pl.pallas_call(
        write_kernel,
        out_shape=(jax.ShapeDtypeStruct(fields.shape, f32), jax.ShapeDtypeStruct(down_state.shape, f32)),
        in_specs=[in_vmem] * len(shapes),
        out_specs=(hbm, hbm),
        scratch_shapes=[vmem(fields.shape[1:], f32), vmem(chunked, f32), dma((14,))],
        compiler_params=pltpu.CompilerParams(vmem_limit_bytes=16 * 1024 * 1024),
        name="write_out",
    )(*middle)


def solution(mesh):
    placed = (
        P("scen", "near", "sect", None),
        P("scen", "near", "sect"),
        P("scen"),
        P("scen"),
        P(),
        P("sect", None),
        P(None, "sect"),
        P(None, None, "sect"),
        P("near"),
    )
    return jax.shard_map(
        body,
        mesh=mesh,
        in_specs=placed,
        out_specs=(P("scen", "near", "sect", None), P("scen", "near", "sect")),
        check_vma=False,
    )
```
